512 devices in a mesh: grp: 8 (over x, core), wide: 64 (over z, y).
Axes of the slice: x: 4, y: 4, z: 16, core: 2. Of those that a mesh axis runs over, the one named last changes fastest.
Arguments:
- anchor_states: bfloat16 [65536, 1024], P(('wide', 'grp')), may hold values from -6 to 6
- key_weight: bfloat16 [1024, 1024], P(None, 'grp'), may hold values from -0.1875 to 0.1875
- value_weight: bfloat16 [1024, 1024], P(None, 'grp'), may hold values from -0.1875 to 0.1875
- panel_query: bfloat16 [131072, 1024], P(('wide', 'grp')), may hold values from -160 to 160
- cell_list: int32 [1024, 4], P('wide'), may hold values from 0 to 7, as said below
- cell_count: int32 [1024], P('wide'), may hold values from 1 to 4, as said below
- norm_gain: float32 [1024], replicated, may hold values from 0.1 to 1.9
- up_weight: bfloat16 [1024, 512], replicated, may hold values from -0.1875 to 0.1875
- flux_weight: bfloat16 [4, 512], replicated, may hold values from -0.25 to 0.25
Outputs:
- flux: float32 [4, 131072], P(None, ('wide', 'grp'))
The draws below stay inside these ranges and needn't reach their ends.
Inputs may be any that keep to these rules, and one draw needn't show every extreme that they name: `cell_list`: the entries of a row are distinct cell blocks of that panel block's region; entries past cell_count are not used. `cell_count`: every region has a panel block whose list uses all 4 slots.
All inputs are finite; a program needn't handle non-finite values.
Results may differ from the reference program's by a relative error of at most 0.007.
Values may be sent and summed in bfloat16 or wider, within the bound.
No kernel may reach another device: no remote copies, remote signals or barrier semaphores. Data moves between devices by JAX's collectives and lax.ppermute only.
A program may use at most 64 MiB of HBM per device.

```python
import math
import jax
import jax.numpy as jnp
from jax import lax

D = 1024
HEADS = 16
FF = 512
NF = 4
BLK = 128
LMAX = 4
HD = 64
ANCHORS = 65536
PANELS = 131072
REGION_ANCHORS = 1024
REGION_PANELS = 2048
SLAB = 32
REGION_BLOCKS = 16
CBLK = 8
NBLK = 1024
N_WIDE = 64


def draw_cell_list(key, part):
    scores = jax.random.randint(key, (NBLK, CBLK), 0, 1 << 20) * CBLK + jnp.arange(CBLK, dtype=jnp.int32)[None, :]
    order = jnp.argsort(scores, axis=1)
    return order[:, :LMAX].astype(jnp.int32)


def draw_cell_count(key, part):
    per_region = NBLK // N_WIDE
    base = jax.random.randint(jax.random.fold_in(key, 1), (NBLK,), 1, LMAX + 1)
    pick = jax.random.randint(jax.random.fold_in(key, 2), (N_WIDE,), 0, per_region)
    rows = jnp.arange(NBLK, dtype=jnp.int32)
    chosen = rows % per_region == pick[rows // per_region]
    return jnp.where(chosen, LMAX, base).astype(jnp.int32)


def draw_panel_query(key, part):
    row_scale = jnp.exp(jax.random.uniform(jax.random.fold_in(key, 3), (PANELS, 1), minval=math.log(0.3), maxval=math.log(3.0)))
    base = jnp.clip(jax.random.normal(jax.random.fold_in(key, 4), (PANELS, D)), -6.0, 6.0)
    scale = row_scale
    return (base * scale).astype(jnp.bfloat16)


def block_scale(key, dims, split, smallest, high):
    def one(dim, parts):
        draws = jax.random.uniform(jax.random.fold_in(jax.random.fold_in(key, 6), dim), (parts,), jnp.float32, smallest / len(split), high / len(split))
        return jnp.repeat(jnp.exp(draws), dims[dim] // parts).reshape((-1,) + (1,) * (len(dims) - dim - 1))

    factor_of = one(*split[0])
    for cut in split[1:]:
        factor_of = factor_of * one(*cut)
    return factor_of


def normal_values(key, extent, deviation, most, cuts=(), held_as=jnp.bfloat16):
    values = deviation * jax.random.normal(key, extent, jnp.float32)
    if cuts:
        values = values * block_scale(key, extent, cuts, -0.22, 0.18)
    return jnp.clip(values, -most, most).astype(held_as)


def setup_inputs(seed: int = 0) -> dict:
    key_of = jax.random.split(jax.random.key(seed), 10)
    return {
        "anchor_states": normal_values(key_of[0], (ANCHORS, D), 1.0, 6.0, ((0, 512),)),
        "key_weight": normal_values(key_of[1], (D, D), D ** -0.5, 0.1875, ((1, 8),)),
        "value_weight": normal_values(key_of[2], (D, D), D ** -0.5, 0.1875, ((1, 8),)),
        "panel_query": draw_panel_query(jax.random.fold_in(key_of[9], 71), 0),
        "cell_list": draw_cell_list(jax.random.fold_in(key_of[9], 71), 0),
        "cell_count": draw_cell_count(jax.random.fold_in(key_of[9], 71), 0),
        "norm_gain": jnp.clip(1.0 + 0.18 * jax.random.normal(key_of[6], (D,), jnp.float32), 0.1, 1.9),
        "up_weight": normal_values(key_of[7], (D, FF), D ** -0.5, 0.1875),
        "flux_weight": normal_values(key_of[8], (NF, FF), FF ** -0.5, 0.25),
    }


def attend_region(region_keys, region_values, region_query, lists, counts):
    key_blocks = region_keys.reshape(CBLK, BLK, HEADS, HD)
    value_blocks = region_values.reshape(CBLK, BLK, HEADS, HD)
    query_blocks = region_query.reshape(REGION_BLOCKS, BLK, HEADS, HD)

    def one_block(item):
        query_block, listed, count = item
        picked_keys = key_blocks[listed].reshape(LMAX * BLK, HEADS, HD).astype(jnp.float32)
        picked_values = value_blocks[listed].reshape(LMAX * BLK, HEADS, HD).astype(jnp.float32)
        scores = jnp.einsum('ihd,jhd->hij', query_block.astype(jnp.float32), picked_keys) / math.sqrt(HD)
        valid = jnp.repeat(jnp.arange(LMAX, dtype=jnp.int32) < count, BLK)
        scores = jnp.where(valid[None, None, :], scores, -jnp.inf)
        top = lax.optimization_barrier(jnp.max(scores, axis=-1, keepdims=True))
        expo = jnp.exp(scores - top)
        weights = (expo / lax.optimization_barrier(jnp.sum(expo, axis=-1, keepdims=True))).astype(jnp.bfloat16)
        output = jnp.einsum('hij,jhd->ihd', weights.astype(jnp.float32), picked_values)
        return output.reshape(BLK, D).astype(jnp.bfloat16)
    return lax.map(one_block, (query_blocks, lists, counts))

def reference(anchor_states, key_weight, value_weight, panel_query, cell_list, cell_count, norm_gain, up_weight, flux_weight):
    keys = jnp.dot(anchor_states, key_weight, preferred_element_type=jnp.float32).astype(jnp.bfloat16)
    anchor_values = jnp.dot(anchor_states, value_weight, preferred_element_type=jnp.float32).astype(jnp.bfloat16)
    region_keys = keys.reshape(N_WIDE, REGION_ANCHORS, D)
    region_values = anchor_values.reshape(N_WIDE, REGION_ANCHORS, D)
    region_query = panel_query.reshape(N_WIDE, N_WIDE, SLAB, D).transpose(1, 0, 2, 3).reshape(N_WIDE, REGION_PANELS, D)
    lists = cell_list.reshape(N_WIDE, REGION_BLOCKS, LMAX)
    counts = cell_count.reshape(N_WIDE, REGION_BLOCKS)

    def one_region(item):
        return attend_region(item[0], item[1], item[2], item[3], item[4])
    attended = lax.map(one_region, (region_keys, region_values, region_query, lists, counts))
    attended = attended.reshape(N_WIDE, N_WIDE, SLAB, D).transpose(1, 0, 2, 3).reshape(PANELS, D)
    stream = panel_query.astype(jnp.float32) + attended.astype(jnp.float32)
    scale = lax.rsqrt(lax.optimization_barrier(jnp.mean(stream * stream, axis=-1, keepdims=True)) + 1e-06)
    normed = (stream * scale * norm_gain.astype(jnp.float32)[None, :]).astype(jnp.bfloat16)
    hidden = jax.nn.gelu(jnp.dot(normed, up_weight, preferred_element_type=jnp.float32)).astype(jnp.bfloat16)
    flux = lax.dot_general(flux_weight, hidden, (((1,), (1,)), ((), ())), preferred_element_type=jnp.float32)
    return flux
```

```python
import functools
import math

import jax
import jax.numpy as jnp
from jax import lax
from jax.experimental import pallas as pl
from jax.experimental.pallas import tpu as pltpu
from jax.sharding import Mesh
from jax.sharding import PartitionSpec as P

BLK = 128
LMAX = 4
HD = 64
SLAB = 32
GRP = ("x", "core")
PLANE = ("x", "core", "y")


def exchange(array, axes):
    return lax.all_to_all(array, axes, split_axis=0, concat_axis=0, tiled=True)


def attend_kernel(cells_ref, counts_ref, query_ref, keys_ref, values_ref, out_ref):
    block = pl.program_id(0)
    parts, _, part_rows, width = out_ref.shape
    slab_part = SLAB // parts
    to_row = lax.broadcasted_iota(jnp.int32, (BLK, BLK), 0)
    from_row = lax.broadcasted_iota(jnp.int32, (BLK, BLK), 1)
    part, rest = to_row // part_rows, to_row % part_rows
    wanted = rest // slab_part * SLAB + part * slab_part + rest % slab_part
    select = (from_row == wanted).astype(jnp.bfloat16)
    query = jnp.dot(select, query_ref[0], preferred_element_type=jnp.float32)
    scaled = query * (1.0 / math.sqrt(HD))
    first = lax.broadcasted_iota(jnp.int32, (BLK, width), 1) < HD
    both = jnp.concatenate(
        [jnp.where(first, scaled, 0.0), jnp.where(first, 0.0, scaled)], axis=0
    ).astype(jnp.bfloat16)
    picked = [
        pl.multiple_of(jnp.clip(cells_ref[block, slot], 0, keys_ref.shape[0] // BLK - 1) * BLK, BLK)
        for slot in range(LMAX)
    ]
    keys = jnp.concatenate([keys_ref[pl.ds(row, BLK), :] for row in picked], axis=0)
    values = jnp.concatenate([values_ref[pl.ds(row, BLK), :] for row in picked], axis=0)
    scores = lax.dot_general(
        both, keys, (((1,), (1,)), ((), ())), preferred_element_type=jnp.float32
    )
    slot_of = lax.broadcasted_iota(jnp.int32, (1, LMAX * BLK), 1) // BLK
    scores = jnp.where(slot_of < counts_ref[block], scores, -jnp.inf)
    top = jnp.max(scores, axis=-1, keepdims=True)
    expo = jnp.exp(scores - top)
    total = jnp.sum(expo, axis=-1, keepdims=True)
    summed = jnp.dot(expo.astype(jnp.bfloat16), values, preferred_element_type=jnp.float32) / total
    attended = jnp.where(first, summed[:BLK], summed[BLK:]).astype(jnp.bfloat16)
    stream = query + attended.astype(jnp.float32)
    out_ref[:, 0] = stream.astype(jnp.bfloat16).reshape(parts, part_rows, width)


def attend(query, keys, values, cells, counts, parts):
    blocks, _, width = query.shape
    part_rows = BLK // parts
    return pl.pallas_call(
        attend_kernel,
        out_shape=jax.ShapeDtypeStruct((parts, blocks, part_rows, width), jnp.bfloat16),
        grid_spec=pltpu.PrefetchScalarGridSpec(
            num_scalar_prefetch=2,
            grid=(blocks,),
            in_specs=[
                pl.BlockSpec((1, BLK, width), lambda i, *_: (i, 0, 0)),
                pl.BlockSpec(keys.shape, lambda i, *_: (0, 0)),
                pl.BlockSpec(values.shape, lambda i, *_: (0, 0)),
            ],
            out_specs=pl.BlockSpec((parts, 1, part_rows, width), lambda i, *_: (0, i, 0, 0)),
        ),
        name="attend",
    )(cells, counts, query, keys, values)


def flux_kernel(stream_ref, gain_ref, up_ref, flux_ref, out_ref):
    groups = stream_ref.shape[0]
    stream = jnp.concatenate(
        [stream_ref[h].astype(jnp.float32) for h in range(groups)], axis=1
    )
    scale = lax.rsqrt(jnp.mean(stream * stream, axis=-1, keepdims=True) + 1e-06)
    normed = (stream * scale * gain_ref[...]).astype(jnp.bfloat16)
    hidden = jax.nn.gelu(
        jnp.dot(normed, up_ref[...], preferred_element_type=jnp.float32)
    ).astype(jnp.bfloat16)
    out_ref[...] = lax.dot_general(
        flux_ref[...], hidden, (((1,), (1,)), ((), ())), preferred_element_type=jnp.float32
    )


def wall_flux(stream, norm_gain, up_weight, flux_weight):
    rows = stream.shape[1]
    return pl.pallas_call(
        flux_kernel,
        out_shape=jax.ShapeDtypeStruct((flux_weight.shape[0], rows), jnp.float32),
        name="wall_flux",
    )(stream, norm_gain[None, :], up_weight, flux_weight)


def body(
    sizes,
    anchor_states,
    key_weight,
    value_weight,
    panel_query,
    cell_list,
    cell_count,
    norm_gain,
    up_weight,
    flux_weight,
):
    grp, n_z, n_y = sizes
    region_anchors = lax.all_gather(anchor_states, GRP, axis=0, tiled=True)
    width = key_weight.shape[1]
    hi = n_z // grp
    query = panel_query.reshape(hi, n_y, SLAB, grp, width).transpose(3, 1, 0, 2, 4)
    query = exchange(query.reshape(grp * n_y, hi * SLAB, width), PLANE)
    query = query.reshape(grp, n_y, hi, SLAB, width).transpose(0, 2, 1, 3, 4)
    query = exchange(query.reshape(n_z, n_y * SLAB, width), "z")
    keys = jnp.dot(region_anchors, key_weight, preferred_element_type=jnp.float32)
    values = jnp.dot(region_anchors, value_weight, preferred_element_type=jnp.float32)
    stream = attend(
        query, keys.astype(jnp.bfloat16), values.astype(jnp.bfloat16), cell_list, cell_count, grp
    )
    stream = exchange(stream, GRP)
    flux = wall_flux(stream.reshape(grp, -1, width), norm_gain, up_weight, flux_weight)
    parts = flux.shape[0]
    few = SLAB // grp
    flux = exchange(flux.reshape(parts, n_z, n_y * few).transpose(1, 0, 2), "z")
    flux = flux.reshape(grp, hi, parts, n_y, few).transpose(0, 3, 1, 2, 4)
    flux = exchange(flux.reshape(grp * n_y, hi * parts, few), PLANE)
    flux = flux.reshape(grp, n_y, hi, parts, few).transpose(3, 2, 1, 0, 4)
    return flux.reshape(parts, -1)


def solution(mesh):
    grp, wide = mesh.devices.shape
    sizes = (grp, 16, wide // 16)
    fine = Mesh(mesh.devices.reshape(grp // 2, 2, 16, wide // 16), ("x", "core", "z", "y"))
    rows = ("z", "y", "x", "core")
    in_specs = (
        P(rows, None),
        P(None, GRP),
        P(None, GRP),
        P(rows, None),
        P(("z", "y"), None),
        P(("z", "y")),
        P(),
        P(),
        P(),
    )
    return jax.shard_map(
        functools.partial(body, sizes),
        mesh=fine,
        in_specs=in_specs,
        out_specs=P(None, rows),
        check_vma=False,
    )
```

```python
import functools
import math

import jax
import jax.numpy as jnp
from jax import lax
from jax.experimental import pallas as pl
from jax.experimental.pallas import tpu as pltpu
from jax.sharding import Mesh
from jax.sharding import PartitionSpec as P

BLK = 128
LMAX = 4
HD = 64
SLAB = 32
GRP = ("x", "core")
PLANE = ("x", "core", "y")


def exchange(array, axes):
    return lax.all_to_all(array, axes, split_axis=0, concat_axis=0, tiled=True)


def attend_step(step, per, place_ref, cells_ref, counts_ref, query_ref, kv_ref, out_ref):
    parts, _, part_rows, width = out_ref.shape
    cells = kv_ref.shape[0] // BLK
    first = lax.broadcasted_iota(jnp.int32, (BLK, width), 1) < HD
    for item in range(per):
        block = step * per + item
        query = query_ref[block].astype(jnp.float32)
        scaled = query * (1.0 / math.sqrt(HD))
        both = jnp.concatenate(
            [jnp.where(first, scaled, 0.0), jnp.where(first, 0.0, scaled)], axis=0
        ).astype(jnp.bfloat16)
        picked = []
        for slot in range(LMAX):
            cell = jnp.clip(cells_ref[block * LMAX + slot], 0, cells - 1)
            far = (cell // 2 - place_ref[0] + cells) % (cells // 2)
            row = far + (cells // 2) * ((cell + place_ref[1]) % 2)
            picked.append(pl.multiple_of(row * BLK, BLK))
        keys = jnp.concatenate([kv_ref[pl.ds(row, BLK), :width] for row in picked], axis=0)
        values = jnp.concatenate([kv_ref[pl.ds(row, BLK), width:] for row in picked], axis=0)
        scores = lax.dot_general(
            both, keys, (((1,), (1,)), ((), ())), preferred_element_type=jnp.float32
        )
        slot_of = lax.broadcasted_iota(jnp.int32, (1, LMAX * BLK), 1) // BLK
        scores = scores + jnp.where(slot_of < counts_ref[block], 0.0, -jnp.inf)
        top = jnp.max(scores, axis=-1, keepdims=True)
        expo = jnp.exp(scores - top)
        total = jnp.sum(expo, axis=-1, keepdims=True)
        summed = jnp.dot(expo.astype(jnp.bfloat16), values, preferred_element_type=jnp.float32)
        summed = summed / total
        attended = jnp.where(first, summed[:BLK], summed[BLK:]).astype(jnp.bfloat16)
        stream = query + attended.astype(jnp.float32)
        out_ref[:, block] = stream.astype(jnp.bfloat16).reshape(parts, part_rows, width)


def attend_kernel(per, *refs):
    steps = refs[3].shape[0] // per
    lax.fori_loop(0, steps, lambda step, _: attend_step(step, per, *refs), None)


def attend(query, kv, place, cells, counts, parts, per):
    blocks, _, width = query.shape
    return pl.pallas_call(
        functools.partial(attend_kernel, per),
        out_shape=jax.ShapeDtypeStruct((parts, blocks, BLK // parts, width), jnp.bfloat16),
        in_specs=[pl.BlockSpec(memory_space=pltpu.SMEM)] * 3
        + [pl.BlockSpec(memory_space=pltpu.VMEM)] * 2,
        out_specs=pl.BlockSpec(memory_space=pltpu.VMEM),
        name="attend",
    )(place, cells, counts, query, kv)


def flux_kernel(stream_ref, gain_ref, up_ref, flux_ref, out_ref):
    groups = stream_ref.shape[0]
    stream = jnp.concatenate(
        [stream_ref[h].astype(jnp.float32) for h in range(groups)], axis=1
    )
    scale = lax.rsqrt(jnp.mean(stream * stream, axis=-1, keepdims=True) + 1e-06)
    normed = (stream * scale * gain_ref[...]).astype(jnp.bfloat16)
    hidden = jax.nn.gelu(
        jnp.dot(normed, up_ref[...], preferred_element_type=jnp.float32)
    ).astype(jnp.bfloat16)
    flux = lax.dot_general(
        flux_ref[...], hidden, (((1,), (1,)), ((), ())), preferred_element_type=jnp.float32
    )
    for block in range(out_ref.shape[0]):
        few = out_ref.shape[2]
        out_ref[block] = flux[:, block * few : (block + 1) * few]


def wall_flux(stream, norm_gain, up_weight, flux_weight, blocks):
    few = stream.shape[1] // blocks
    return pl.pallas_call(
        flux_kernel,
        out_shape=jax.ShapeDtypeStruct((blocks, flux_weight.shape[0], few), jnp.float32),
        name="wall_flux",
    )(stream, norm_gain[None, :], up_weight, flux_weight)


def place_kernel(y_ref, flux_ref, out_ref):
    _, halves, n_y, both, few = flux_ref.shape
    comps = out_ref.shape[0]
    mine = flux_ref[y_ref[0]]
    pieces = [
        mine[half, low, top * comps : (top + 1) * comps]
        for top in range(both // comps)
        for low in range(n_y)
        for half in range(halves)
    ]
    out_ref[...] = jnp.concatenate(pieces, axis=1)


def place_flux(flux, comps, y):
    return pl.pallas_call(
        place_kernel,
        out_shape=jax.ShapeDtypeStruct((comps, flux[0].size // comps), jnp.float32),
        in_specs=[
            pl.BlockSpec(memory_space=pltpu.SMEM),
            pl.BlockSpec(memory_space=pltpu.VMEM),
        ],
        name="place_flux",
    )(y, flux)


def body(
    sizes,
    anchor_states,
    key_weight,
    value_weight,
    panel_query,
    cell_list,
    cell_count,
    norm_gain,
    up_weight,
    flux_weight,
):
    n_x, n_z, n_y = sizes
    grp = 2 * n_x
    width = key_weight.shape[1]
    hi = n_z // grp
    query = panel_query.reshape(hi, n_y, SLAB, grp, width).transpose(3, 1, 0, 2, 4)
    query = exchange(query.reshape(grp * n_y, hi * SLAB, width), PLANE)
    query = query.reshape(grp, n_y, hi, SLAB, width).transpose(0, 2, 1, 3, 4)
    query = query.reshape(n_z, n_y * SLAB, width)
    query, anchors = lax.optimization_barrier((query, anchor_states))
    query = exchange(query, "z")
    along = [anchors] + [
        lax.ppermute(anchors, "x", [((i + far) % n_x, i) for i in range(n_x)])
        for far in range(1, n_x)
    ]
    along = jnp.concatenate(along, axis=0)
    across = lax.ppermute(along, "core", [(0, 1), (1, 0)])
    weights = jnp.concatenate([key_weight, value_weight], axis=1)
    kv = jnp.concatenate(
        [
            jnp.dot(part, weights, preferred_element_type=jnp.float32).astype(jnp.bfloat16)
            for part in (along, across)
        ],
        axis=0,
    )
    place = jnp.stack([lax.axis_index("x"), lax.axis_index("core")]).astype(jnp.int32)
    stream = attend(query, kv, place, cell_list.reshape(-1), cell_count, grp, 4)
    stream = exchange(stream, GRP)
    flux = wall_flux(
        stream.reshape(grp, -1, width), norm_gain, up_weight, flux_weight, n_z
    )
    comps = flux_weight.shape[0]
    few = flux.shape[2]
    flux = exchange(flux, "z").reshape(grp, 1, hi * comps, few)
    flux = jnp.broadcast_to(flux, (grp, n_y, hi * comps, few))
    flux = exchange(flux.reshape(grp * n_y, hi * comps, few), PLANE)
    return place_flux(
        flux.reshape(n_x, 2, n_y, hi * comps, few), comps, lax.axis_index("y").reshape(1)
    )


def solution(mesh):
    grp, wide = mesh.devices.shape
    sizes = (grp // 2, 16, wide // 16)
    fine = Mesh(mesh.devices.reshape(grp // 2, 2, 16, wide // 16), ("x", "core", "z", "y"))
    rows = ("z", "y", "x", "core")
    in_specs = (
        P(rows, None),
        P(None, GRP),
        P(None, GRP),
        P(rows, None),
        P(("z", "y"), None),
        P(("z", "y")),
        P(),
        P(),
        P(),
    )
    return jax.shard_map(
        functools.partial(body, sizes),
        mesh=fine,
        in_specs=in_specs,
        out_specs=P(None, rows),
        check_vma=False,
    )
```

```python
import functools
import math

import jax
import jax.numpy as jnp
from jax import lax
from jax.experimental import pallas as pl
from jax.experimental.pallas import tpu as pltpu
from jax.sharding import Mesh
from jax.sharding import PartitionSpec as P

BLK = 128
LMAX = 4
HD = 64
SLAB = 32
LANES = 128
GRP = ("x", "core")
PLANE = ("x", "core", "y")


def exchange(array, axes):
    return lax.all_to_all(array, axes, split_axis=0, concat_axis=0, tiled=True)


def on_chip(*arrays):
    return [pltpu.with_memory_space_constraint(array, pltpu.VMEM) for array in arrays]


def attend_step(step, per, place_ref, cells_ref, counts_ref, query_ref, kv_ref, out_ref):
    parts, _, part_rows, width = out_ref.shape
    cells = kv_ref.shape[0] // BLK
    first = lax.broadcasted_iota(jnp.int32, (BLK, width), 1) < HD
    for item in range(per):
        block = step * per + item
        query = query_ref[block].astype(jnp.float32)
        scaled = query * (1.0 / math.sqrt(HD))
        both = jnp.concatenate(
            [jnp.where(first, scaled, 0.0), jnp.where(first, 0.0, scaled)], axis=0
        ).astype(jnp.bfloat16)
        picked = []
        for slot in range(LMAX):
            cell = jnp.clip(cells_ref[block * LMAX + slot], 0, cells - 1)
            far = (cell // 2 - place_ref[0] + cells) % (cells // 2)
            row = far + (cells // 2) * ((cell + place_ref[1]) % 2)
            picked.append(pl.multiple_of(row * BLK, BLK))
        keys = jnp.concatenate([kv_ref[pl.ds(row, BLK), :width] for row in picked], axis=0)
        values = jnp.concatenate([kv_ref[pl.ds(row, BLK), width:] for row in picked], axis=0)
        scores = lax.dot_general(
            both, keys, (((1,), (1,)), ((), ())), preferred_element_type=jnp.float32
        )
        slot_of = lax.broadcasted_iota(jnp.int32, (1, LMAX * BLK), 1) // BLK
        scores = scores + jnp.where(slot_of < counts_ref[block], 0.0, -jnp.inf)
        top = jnp.max(scores, axis=-1, keepdims=True)
        expo = jnp.exp(scores - top)
        total = jnp.sum(expo, axis=-1, keepdims=True)
        summed = jnp.dot(expo.astype(jnp.bfloat16), values, preferred_element_type=jnp.float32)
        summed = summed / total
        attended = jnp.where(first, summed[:BLK], summed[BLK:]).astype(jnp.bfloat16)
        stream = query + attended.astype(jnp.float32)
        out_ref[:, block] = stream.astype(jnp.bfloat16).reshape(parts, part_rows, width)


def attend_kernel(per, *refs):
    steps = refs[3].shape[0] // per
    lax.fori_loop(0, steps, lambda step, _: attend_step(step, per, *refs), None)


def attend(query, kv, place, cells, counts, parts, per):
    blocks, _, width = query.shape
    return pl.pallas_call(
        functools.partial(attend_kernel, per),
        out_shape=pltpu.VMEM((parts, blocks, BLK // parts, width), jnp.bfloat16),
        in_specs=[pl.BlockSpec(memory_space=pltpu.SMEM)] * 3
        + [pl.BlockSpec(memory_space=pltpu.VMEM)] * 2,
        name="attend",
    )(place, cells, counts, *on_chip(query, kv))


def flux_kernel(stream_ref, gain_ref, up_ref, flux_ref, out_ref):
    groups = stream_ref.shape[0]
    stream = jnp.concatenate(
        [stream_ref[h].astype(jnp.float32) for h in range(groups)], axis=1
    )
    scale = lax.rsqrt(jnp.mean(stream * stream, axis=-1, keepdims=True) + 1e-06)
    normed = (stream * scale * gain_ref[...]).astype(jnp.bfloat16)
    hidden = jax.nn.gelu(
        jnp.dot(normed, up_ref[...], preferred_element_type=jnp.float32)
    ).astype(jnp.bfloat16)
    flux = lax.dot_general(
        flux_ref[...], hidden, (((1,), (1,)), ((), ())), preferred_element_type=jnp.float32
    )
    blocks = out_ref.shape[0]
    few = flux.shape[1] // blocks
    for block in range(blocks):
        piece = flux[:, block * few : (block + 1) * few]
        out_ref[block] = jnp.concatenate([piece] * (LANES // few), axis=1)


def wall_flux(stream, norm_gain, up_weight, flux_weight, blocks):
    return pl.pallas_call(
        flux_kernel,
        out_shape=pltpu.VMEM((blocks, flux_weight.shape[0], LANES), jnp.float32),
        in_specs=[pl.BlockSpec(memory_space=pltpu.VMEM)] * 4,
        name="wall_flux",
    )(*on_chip(stream, norm_gain[None, :], up_weight, flux_weight))


def place_kernel(y_ref, flux_ref, out_ref):
    _, halves, n_y, both, _ = flux_ref.shape
    comps, rows = out_ref.shape
    few = rows * comps // (halves * n_y * both)
    mine = flux_ref.at[y_ref[0]]
    pieces = [
        mine[half, low, top * comps : (top + 1) * comps, :few]
        for top in range(both // comps)
        for low in range(n_y)
        for half in range(halves)
    ]
    out_ref[...] = jnp.concatenate(pieces, axis=1)


def place_flux(flux, comps, rows, y):
    return pl.pallas_call(
        place_kernel,
        out_shape=jax.ShapeDtypeStruct((comps, rows), jnp.float32),
        in_specs=[
            pl.BlockSpec(memory_space=pltpu.SMEM),
            pl.BlockSpec(memory_space=pltpu.VMEM),
        ],
        name="place_flux",
    )(y, *on_chip(flux))


def body(
    sizes,
    anchor_states,
    key_weight,
    value_weight,
    panel_query,
    cell_list,
    cell_count,
    norm_gain,
    up_weight,
    flux_weight,
):
    n_x, n_z, n_y = sizes
    grp = 2 * n_x
    width = key_weight.shape[1]
    hi = n_z // grp
    query = panel_query.reshape(hi, n_y, SLAB, grp, width).transpose(3, 1, 0, 2, 4)
    query = exchange(query.reshape(grp * n_y, hi * SLAB, width), PLANE)
    query = query.reshape(grp, n_y, hi, SLAB, width).transpose(0, 2, 1, 3, 4)
    query = query.reshape(n_z, n_y * SLAB, width)
    query = exchange(query, "z")
    up = [((i + 1) % n_x, i) for i in range(n_x)]
    down = [(i, (i + 1) % n_x) for i in range(n_x)]
    one_up = lax.ppermute(anchor_states, "x", up)
    one_down = lax.ppermute(anchor_states, "x", down)
    two_up = lax.ppermute(one_up, "x", up)
    along = jnp.concatenate([anchor_states, one_up, two_up, one_down], axis=0)
    across = lax.ppermute(along, "core", [(0, 1), (1, 0)])
    weights = jnp.concatenate([key_weight, value_weight], axis=1)
    kv = jnp.concatenate(
        [
            jnp.dot(part, weights, preferred_element_type=jnp.float32).astype(jnp.bfloat16)
            for part in (along, across)
        ],
        axis=0,
    )
    place = jnp.stack([lax.axis_index("x"), lax.axis_index("core")]).astype(jnp.int32)
    stream = attend(query, kv, place, cell_list.reshape(-1), cell_count, grp, 4)
    stream = exchange(stream, GRP)
    flux = wall_flux(
        stream.reshape(grp, -1, width), norm_gain, up_weight, flux_weight, n_z
    )
    comps = flux_weight.shape[0]
    flux = exchange(flux, "z").reshape(grp, 1, hi * comps, LANES)
    flux = jnp.broadcast_to(flux, (grp, n_y, hi * comps, LANES))
    flux = exchange(flux.reshape(grp * n_y, hi * comps, LANES), PLANE)
    return place_flux(
        flux.reshape(n_x, 2, n_y, hi * comps, LANES),
        comps,
        panel_query.shape[0],
        lax.axis_index("y").reshape(1),
    )


def solution(mesh):
    grp, wide = mesh.devices.shape
    sizes = (grp // 2, 16, wide // 16)
    fine = Mesh(mesh.devices.reshape(grp // 2, 2, 16, wide // 16), ("x", "core", "z", "y"))
    rows = ("z", "y", "x", "core")
    in_specs = (
        P(rows, None),
        P(None, GRP),
        P(None, GRP),
        P(rows, None),
        P(("z", "y"), None),
        P(("z", "y")),
        P(),
        P(),
        P(),
    )
    return jax.shard_map(
        functools.partial(body, sizes),
        mesh=fine,
        in_specs=in_specs,
        out_specs=P(None, rows),
        check_vma=False,
    )
```

```python
import functools
import math

import jax
import jax.numpy as jnp
from jax import lax
from jax.experimental import pallas as pl
from jax.experimental.pallas import tpu as pltpu
from jax.sharding import Mesh
from jax.sharding import PartitionSpec as P

BLK = 128
LMAX = 4
HD = 64
SLAB = 32
LANES = 128
GRP = ("x", "core")
PLANE = ("x", "core", "y")


def exchange(array, axes):
    return lax.all_to_all(array, axes, split_axis=0, concat_axis=0, tiled=True)


def on_chip(*arrays):
    return [pltpu.with_memory_space_constraint(array, pltpu.VMEM) for array in arrays]


def specs(scalars, arrays):
    return [pl.BlockSpec(memory_space=pltpu.SMEM)] * scalars + [
        pl.BlockSpec(memory_space=pltpu.VMEM)
    ] * arrays


def project_kernel(place_ref, own_ref, up_ref, down_ref, two_ref, last_ref, across_ref, kv_ref,
                   anchors_ref, weights_ref):
    depth, width = weights_ref.shape[0], own_ref.shape[1]
    parts = depth // width
    rows = parts * BLK
    n_x = weights_ref.shape[1] // width
    pieces = [own_ref, up_ref, two_ref, down_ref]
    for far, ref in enumerate(pieces):
        for part in range(parts):
            lanes = slice(part * width, (part + 1) * width)
            anchors_ref[far * BLK : (far + 1) * BLK, lanes] = ref[part * BLK : (part + 1) * BLK, :]
            start = far * rows + part * BLK
            anchors_ref[(n_x + far) * BLK : (n_x + far + 1) * BLK, lanes] = across_ref[
                start : start + BLK, :
            ]
    for far, ref in enumerate(pieces):
        at = (place_ref[0] + far) % n_x
        lanes = pl.ds(pl.multiple_of(at * width, width), width)
        if ref is two_ref:
            held = ref.shape[0] - rows
            weights_ref[:held, lanes] = ref[rows:, :]
            weights_ref[held:, lanes] = last_ref[...]
        else:
            weights_ref[:, lanes] = ref[rows:, :]
    step = 2 * BLK
    for start in range(0, kv_ref.shape[0], step):
        kv_ref[start : start + step, :] = jnp.dot(
            anchors_ref[start : start + step, :],
            weights_ref[...],
            preferred_element_type=jnp.float32,
        ).astype(jnp.bfloat16)


def project(place, own, up, down, two, last, across, depth, n_x):
    width = own.shape[1]
    return pl.pallas_call(
        project_kernel,
        out_shape=pltpu.VMEM((2 * n_x * BLK, n_x * width), jnp.bfloat16),
        in_specs=specs(1, 6),
        scratch_shapes=[
            pltpu.VMEM((2 * n_x * BLK, depth), jnp.bfloat16),
            pltpu.VMEM((depth, n_x * width), jnp.bfloat16),
        ],
        name="project",
    )(place, own, up, down, two, last, across)


def attend_step(step, per, place_ref, cells_ref, counts_ref, query_ref, kv_ref, keep_ref, send_ref):
    rows, width = query_ref.shape[1:]
    half = rows // 2
    cells = kv_ref.shape[0] // BLK
    quad = 2 * LANES
    heads = quad // HD
    head_of = lax.broadcasted_iota(jnp.int32, (rows, quad), 1) // HD
    for item in range(per):
        block = step * per + item
        picked = []
        for slot in range(LMAX):
            cell = jnp.clip(cells_ref[block * LMAX + slot], 0, cells - 1)
            far = (cell // 2 - place_ref[0] + cells) % (cells // 2)
            row = far + (cells // 2) * ((cell + place_ref[1]) % 2)
            picked.append(pl.multiple_of(row * BLK, BLK))
        slot_of = lax.broadcasted_iota(jnp.int32, (1, LMAX * BLK), 1) // BLK
        bias = jnp.where(slot_of < counts_ref[block], 0.0, -jnp.inf)

        def gathered(first, start):
            lanes = [slice(first + far * quad + start, first + far * quad + start + LANES)
                     for far in range(2)]
            return jnp.concatenate(
                [
                    jnp.concatenate([kv_ref[pl.ds(row, BLK), part] for part in lanes], axis=1)
                    for row in picked
                ],
                axis=0,
            )

        for lane in range(0, width, quad):
            query = query_ref[block, :, lane : lane + quad].astype(jnp.float32)
            scaled = query * (1.0 / math.sqrt(HD))
            each = jnp.concatenate(
                [jnp.where(head_of == head, scaled, 0.0) for head in range(heads)], axis=0
            ).astype(jnp.bfloat16)
            scores = lax.dot_general(
                each,
                gathered(2 * lane, 0),
                (((1,), (1,)), ((), ())),
                preferred_element_type=jnp.float32,
            )
            scores = scores + bias
            top = jnp.max(scores, axis=-1, keepdims=True)
            expo = jnp.exp(scores - top)
            total = jnp.sum(expo, axis=-1, keepdims=True)
            summed = jnp.dot(
                expo.astype(jnp.bfloat16),
                gathered(2 * lane, LANES),
                preferred_element_type=jnp.float32,
            )
            summed = summed / total
            attended = summed[:rows]
            for head in range(1, heads):
                attended = jnp.where(
                    head_of == head, summed[head * rows : (head + 1) * rows], attended
                )
            attended = attended.astype(jnp.bfloat16).astype(jnp.float32)
            stream = (query + attended).astype(jnp.bfloat16)
            low, high = stream[:half], stream[half:]
            keep_ref[block, :, lane : lane + quad] = jnp.where(place_ref[1] == 0, low, high)
            send_ref[block, :, lane : lane + quad] = jnp.where(place_ref[1] == 0, high, low)


def attend_kernel(per, *refs):
    steps = refs[3].shape[0] // per
    lax.fori_loop(0, steps, lambda step, _: attend_step(step, per, *refs), None)


def attend(query, kv, place, cells, counts, per):
    blocks, rows, width = query.shape
    return pl.pallas_call(
        functools.partial(attend_kernel, per),
        out_shape=[pltpu.VMEM((blocks, rows // 2, width), jnp.bfloat16)] * 2,
        in_specs=specs(3, 2),
        name="attend",
    )(place, cells, counts, *on_chip(query, kv))


def flux_kernel(place_ref, mine_ref, other_ref, gain_ref, up_ref, flux_ref, out_ref):
    rows = mine_ref.shape[0]
    core = place_ref[1]
    n_x = gain_ref.shape[0] // 2
    mine = mine_ref[...].astype(jnp.float32)
    other = other_ref[...].astype(jnp.float32)
    squares = jnp.sum(mine * mine, axis=-1, keepdims=True) + jnp.sum(
        other * other, axis=-1, keepdims=True
    )
    scale = lax.rsqrt(squares / (mine.shape[1] + other.shape[1]) + 1e-06)
    hidden = jnp.zeros((rows, up_ref.shape[2]), jnp.float32)
    for stream, at in ((mine, core), (other, 1 - core)):
        gain = jnp.concatenate([gain_ref[2 * x + at] for x in range(n_x)], axis=1)
        weights = jnp.concatenate([up_ref[2 * x + at] for x in range(n_x)], axis=0)
        normed = (stream * scale * gain).astype(jnp.bfloat16)
        hidden = hidden + jnp.dot(normed, weights, preferred_element_type=jnp.float32)
    hidden = jax.nn.gelu(hidden).astype(jnp.bfloat16)
    flux = lax.dot_general(
        flux_ref[...], hidden, (((1,), (1,)), ((), ())), preferred_element_type=jnp.float32
    )
    blocks = out_ref.shape[0]
    few = rows // blocks
    for block in range(blocks):
        piece = flux[:, block * few : (block + 1) * few]
        out_ref[block] = jnp.concatenate([piece] * (LANES // few), axis=1)


def wall_flux(place, mine, other, norm_gain, up_weight, flux_weight, blocks):
    groups = norm_gain.shape[0] // LANES
    return pl.pallas_call(
        flux_kernel,
        out_shape=pltpu.VMEM((blocks, flux_weight.shape[0], LANES), jnp.float32),
        in_specs=specs(1, 5),
        name="wall_flux",
    )(
        place,
        *on_chip(
            mine,
            other,
            norm_gain.reshape(groups, 1, LANES),
            up_weight.reshape(groups, LANES, -1),
            flux_weight,
        ),
    )


def place_kernel(y_ref, flux_ref, out_ref):
    n_x, halves, n_y, both, _ = flux_ref.shape
    comps = out_ref.shape[0]
    few = SLAB // n_x
    core = y_ref[0] // (n_y // halves)
    even = y_ref[0] % (n_y // halves) == 0
    pieces = []
    for top in range(both // comps):
        for low in range(n_y):
            for x in range(n_x):
                piece = flux_ref[x, core, low, top * comps : (top + 1) * comps]
                pieces.append(jnp.where(even, piece[:, :few], piece[:, few : 2 * few]))
    out_ref[...] = jnp.concatenate(pieces, axis=1)


def place_flux(flux, comps, rows, y):
    return pl.pallas_call(
        place_kernel,
        out_shape=jax.ShapeDtypeStruct((comps, rows), jnp.float32),
        in_specs=specs(1, 1),
        name="place_flux",
    )(y, *on_chip(flux))


def body(
    sizes,
    anchor_states,
    key_weight,
    value_weight,
    panel_query,
    cell_list,
    cell_count,
    norm_gain,
    up_weight,
    flux_weight,
):
    n_x, n_z, n_y = sizes
    grp = 2 * n_x
    depth, width = key_weight.shape
    few = SLAB // n_x
    half = n_x * width
    hi = n_z // grp
    query = panel_query.reshape(hi, n_y, n_x, few, n_x, 2, width).transpose(2, 5, 1, 0, 3, 4, 6)
    query = exchange(query.reshape(grp * n_y, hi * few, half), PLANE)
    query = query.reshape(grp, n_y, hi, few, half).transpose(0, 2, 1, 3, 4)
    query = exchange(query.reshape(n_z, n_y * few, half), "z")
    weights = jnp.concatenate([key_weight, value_weight], axis=1)
    cut = depth // (2 * width)
    anchors = anchor_states.reshape(BLK, cut, 2 * width).transpose(1, 0, 2)
    rows = cut * BLK
    own = jnp.concatenate([anchors.reshape(rows, 2 * width), weights], axis=0)
    up = [((i + 1) % n_x, i) for i in range(n_x)]
    down = [(i, (i + 1) % n_x) for i in range(n_x)]
    one_up = lax.ppermute(own, "x", up)
    one_down = lax.ppermute(own, "x", down)
    middle = own.shape[0] // 2
    two = lax.ppermute(one_up[:middle], "x", up)
    last = lax.ppermute(one_down[middle:], "x", down)
    two, last = lax.optimization_barrier((two, last))
    along = jnp.concatenate([own[:rows], one_up[:rows], two[:rows], one_down[:rows]], axis=0)
    across = lax.ppermute(along, "core", [(0, 1), (1, 0)])
    place = jnp.stack([lax.axis_index("x"), lax.axis_index("core")]).astype(jnp.int32)
    kv = project(place, own, one_up, one_down, two, last, across, depth, n_x)
    keep, send = attend(query, kv, place, cell_list.reshape(-1), cell_count, 2)
    other = lax.ppermute(send, "core", [(0, 1), (1, 0)])
    flux = wall_flux(
        place,
        keep.reshape(-1, half),
        other.reshape(-1, half),
        norm_gain,
        up_weight,
        flux_weight,
        n_z,
    )
    comps = flux_weight.shape[0]
    flux = exchange(flux, "z").reshape(grp, 1, hi * comps, LANES)
    flux = jnp.broadcast_to(flux, (grp, n_y, hi * comps, LANES))
    flux = exchange(flux.reshape(grp * n_y, hi * comps, LANES), PLANE)
    return place_flux(
        flux.reshape(n_x, 2, n_y, hi * comps, LANES),
        comps,
        panel_query.shape[0],
        lax.axis_index("y").reshape(1),
    )


def solution(mesh):
    grp, wide = mesh.devices.shape
    sizes = (grp // 2, 16, wide // 16)
    fine = Mesh(mesh.devices.reshape(grp // 2, 2, 16, wide // 16), ("x", "core", "z", "y"))
    rows = ("z", "y", "x", "core")
    in_specs = (
        P(rows, None),
        P(None, GRP),
        P(None, GRP),
        P(rows, None),
        P(("z", "y"), None),
        P(("z", "y")),
        P(),
        P(),
        P(),
    )
    return jax.shard_map(
        functools.partial(body, sizes),
        mesh=fine,
        in_specs=in_specs,
        out_specs=P(None, rows),
        check_vma=False,
    )
```

```python
import functools
import math

import jax
import jax.numpy as jnp
from jax import lax
from jax.experimental import pallas as pl
from jax.experimental.pallas import tpu as pltpu
from jax.sharding import Mesh
from jax.sharding import PartitionSpec as P

BLK = 128
LMAX = 4
HD = 64
SLAB = 32
LANES = 128
GRP = ("x", "core")
PLANE = ("x", "core", "y")


def exchange(array, axes):
    return lax.all_to_all(array, axes, split_axis=0, concat_axis=0, tiled=True)


def on_chip(*arrays):
    return [pltpu.with_memory_space_constraint(array, pltpu.VMEM) for array in arrays]


def split_kernel(query_ref, out_ref):
    chunks, rows, width = out_ref.shape
    groups = query_ref.shape[1] // width
    low = chunks // groups
    for chunk in range(chunks):
        lane = chunk // low * width
        for top in range(rows // SLAB):
            row = (top * low + chunk % low) * SLAB
            out_ref[chunk, top * SLAB : (top + 1) * SLAB, :] = query_ref[
                row : row + SLAB, lane : lane + width
            ]


def split_query(query, groups, low):
    rows, width = query.shape
    return pl.pallas_call(
        split_kernel,
        out_shape=pltpu.VMEM((groups * low, rows // low, width // groups), query.dtype),
        in_specs=[pl.BlockSpec(memory_space=pltpu.VMEM)],
        name="split_query",
    )(query)


def attend_step(step, per, place_ref, cells_ref, counts_ref, query_ref, kv_ref, out_ref):
    parts, _, part_rows, width = out_ref.shape
    cells = kv_ref.shape[0] // BLK
    first = lax.broadcasted_iota(jnp.int32, (BLK, width), 1) < HD
    for item in range(per):
        block = step * per + item
        query = query_ref[block].astype(jnp.float32)
        scaled = query * (1.0 / math.sqrt(HD))
        both = jnp.concatenate(
            [jnp.where(first, scaled, 0.0), jnp.where(first, 0.0, scaled)], axis=0
        ).astype(jnp.bfloat16)
        picked = []
        for slot in range(LMAX):
            cell = jnp.clip(cells_ref[block * LMAX + slot], 0, cells - 1)
            far = (cell // 2 - place_ref[0] + cells) % (cells // 2)
            row = far + (cells // 2) * ((cell + place_ref[1]) % 2)
            picked.append(pl.multiple_of(row * BLK, BLK))
        keys = jnp.concatenate([kv_ref[pl.ds(row, BLK), :width] for row in picked], axis=0)
        values = jnp.concatenate([kv_ref[pl.ds(row, BLK), width:] for row in picked], axis=0)
        scores = lax.dot_general(
            both, keys, (((1,), (1,)), ((), ())), preferred_element_type=jnp.float32
        )
        slot_of = lax.broadcasted_iota(jnp.int32, (1, LMAX * BLK), 1) // BLK
        scores = scores + jnp.where(slot_of < counts_ref[block], 0.0, -jnp.inf)
        top = jnp.max(scores, axis=-1, keepdims=True)
        expo = jnp.exp(scores - top)
        total = jnp.sum(expo, axis=-1, keepdims=True)
        summed = jnp.dot(expo.astype(jnp.bfloat16), values, preferred_element_type=jnp.float32)
        summed = summed / total
        attended = jnp.where(first, summed[:BLK], summed[BLK:]).astype(jnp.bfloat16)
        stream = query + attended.astype(jnp.float32)
        out_ref[:, block] = stream.astype(jnp.bfloat16).reshape(parts, part_rows, width)


def attend_kernel(per, *refs):
    steps = refs[3].shape[0] // per
    lax.fori_loop(0, steps, lambda step, _: attend_step(step, per, *refs), None)


def attend(query, kv, place, cells, counts, parts, per):
    blocks, _, width = query.shape
    return pl.pallas_call(
        functools.partial(attend_kernel, per),
        out_shape=pltpu.VMEM((parts, blocks, BLK // parts, width), jnp.bfloat16),
        in_specs=[pl.BlockSpec(memory_space=pltpu.SMEM)] * 3
        + [pl.BlockSpec(memory_space=pltpu.VMEM)] * 2,
        name="attend",
    )(place, cells, counts, *on_chip(query, kv))


def flux_kernel(stream_ref, gain_ref, up_ref, flux_ref, out_ref):
    groups = stream_ref.shape[0]
    stream = jnp.concatenate(
        [stream_ref[h].astype(jnp.float32) for h in range(groups)], axis=1
    )
    scale = lax.rsqrt(jnp.mean(stream * stream, axis=-1, keepdims=True) + 1e-06)
    normed = (stream * scale * gain_ref[...]).astype(jnp.bfloat16)
    hidden = jax.nn.gelu(
        jnp.dot(normed, up_ref[...], preferred_element_type=jnp.float32)
    ).astype(jnp.bfloat16)
    flux = lax.dot_general(
        flux_ref[...], hidden, (((1,), (1,)), ((), ())), preferred_element_type=jnp.float32
    )
    blocks = out_ref.shape[0]
    few = flux.shape[1] // blocks
    for block in range(blocks):
        piece = flux[:, block * few : (block + 1) * few]
        out_ref[block] = jnp.concatenate([piece] * (LANES // few), axis=1)


def wall_flux(stream, norm_gain, up_weight, flux_weight, blocks):
    return pl.pallas_call(
        flux_kernel,
        out_shape=pltpu.VMEM((blocks, flux_weight.shape[0], LANES), jnp.float32),
        in_specs=[pl.BlockSpec(memory_space=pltpu.VMEM)] * 4,
        name="wall_flux",
    )(*on_chip(stream, norm_gain[None, :], up_weight, flux_weight))


def place_kernel(place_ref, flux_ref, out_ref):
    _, halves, n_y, both, _ = flux_ref.shape
    comps, rows = out_ref.shape
    few = rows * comps // (halves * n_y * both)
    mine = flux_ref.at[place_ref[2]]
    pieces = [
        mine[half, low, top * comps : (top + 1) * comps, :few]
        for top in range(both // comps)
        for low in range(n_y)
        for half in range(halves)
    ]
    out_ref[...] = jnp.concatenate(pieces, axis=1)


def place_flux(place, flux, comps, rows):
    return pl.pallas_call(
        place_kernel,
        out_shape=jax.ShapeDtypeStruct((comps, rows), jnp.float32),
        in_specs=[
            pl.BlockSpec(memory_space=pltpu.SMEM),
            pl.BlockSpec(memory_space=pltpu.VMEM),
        ],
        name="place_flux",
    )(place, *on_chip(flux))


def body(
    sizes,
    anchor_states,
    key_weight,
    value_weight,
    panel_query,
    cell_list,
    cell_count,
    norm_gain,
    up_weight,
    flux_weight,
):
    n_x, n_z, n_y = sizes
    grp = 2 * n_x
    width = key_weight.shape[1]
    hi = n_z // grp
    query = exchange(split_query(panel_query, grp, n_y), PLANE)
    query = query.reshape(grp, n_y, hi, SLAB, width).transpose(0, 2, 1, 3, 4)
    query = query.reshape(n_z, n_y * SLAB, width)
    query = exchange(query, "z")
    up = [((i + 1) % n_x, i) for i in range(n_x)]
    down = [(i, (i + 1) % n_x) for i in range(n_x)]
    one_up = lax.ppermute(anchor_states, "x", up)
    one_down = lax.ppermute(anchor_states, "x", down)
    two_up = lax.ppermute(one_up, "x", up)
    along = jnp.concatenate([anchor_states, one_up, two_up, one_down], axis=0)
    across = lax.ppermute(along, "core", [(0, 1), (1, 0)])
    weights = jnp.concatenate([key_weight, value_weight], axis=1)
    kv = jnp.concatenate(
        [
            jnp.dot(part, weights, preferred_element_type=jnp.float32).astype(jnp.bfloat16)
            for part in (along, across)
        ],
        axis=0,
    )
    place = jnp.stack([lax.axis_index(axis) for axis in PLANE]).astype(jnp.int32)
    stream = attend(query, kv, place, cell_list.reshape(-1), cell_count, grp, 16)
    stream = exchange(stream, GRP)
    flux = wall_flux(
        stream.reshape(grp, -1, width), norm_gain, up_weight, flux_weight, n_z
    )
    comps = flux_weight.shape[0]
    flux = exchange(flux, "z").reshape(grp, 1, hi * comps, LANES)
    flux = jnp.broadcast_to(flux, (grp, n_y, hi * comps, LANES))
    flux = exchange(flux.reshape(grp * n_y, hi * comps, LANES), PLANE)
    return place_flux(
        place, flux.reshape(n_x, 2, n_y, hi * comps, LANES), comps, panel_query.shape[0]
    )


def solution(mesh):
    grp, wide = mesh.devices.shape
    sizes = (grp // 2, 16, wide // 16)
    fine = Mesh(mesh.devices.reshape(grp // 2, 2, 16, wide // 16), ("x", "core", "z", "y"))
    rows = ("z", "y", "x", "core")
    in_specs = (
        P(rows, None),
        P(None, GRP),
        P(None, GRP),
        P(rows, None),
        P(("z", "y"), None),
        P(("z", "y")),
        P(),
        P(),
        P(),
    )
    return jax.shard_map(
        functools.partial(body, sizes),
        mesh=fine,
        in_specs=in_specs,
        out_specs=P(None, rows),
        check_vma=False,
    )
```

```python
import functools
import math

import jax
import jax.numpy as jnp
from jax import lax
from jax.experimental import pallas as pl
from jax.experimental.pallas import tpu as pltpu
from jax.sharding import Mesh
from jax.sharding import PartitionSpec as P

BLK = 128
LMAX = 4
HD = 64
SLAB = 32
LANES = 128
GRP = ("x", "core")
PLANE = ("x", "core", "y")


def exchange(array, axes):
    return lax.all_to_all(array, axes, split_axis=0, concat_axis=0, tiled=True)


def on_chip(*arrays):
    return [pltpu.with_memory_space_constraint(array, pltpu.VMEM) for array in arrays]


def attend_step(step, per, cells_ref, counts_ref, query_ref, kv_ref, out_ref):
    parts, _, part_rows, width = out_ref.shape
    cells = kv_ref.shape[0] // BLK
    x, core = lax.axis_index("x"), lax.axis_index("core")
    first = lax.broadcasted_iota(jnp.int32, (BLK, width), 1) < HD
    for item in range(per):
        block = step * per + item
        query = query_ref[block].astype(jnp.float32)
        scaled = query * (1.0 / math.sqrt(HD))
        both = jnp.concatenate(
            [jnp.where(first, scaled, 0.0), jnp.where(first, 0.0, scaled)], axis=0
        ).astype(jnp.bfloat16)
        picked = []
        for slot in range(LMAX):
            cell = jnp.clip(cells_ref[slot, block], 0, cells - 1)
            far = (cell // 2 - x + cells) % (cells // 2)
            row = far + (cells // 2) * ((cell + core) % 2)
            picked.append(pl.multiple_of(row * BLK, BLK))
        keys = jnp.concatenate([kv_ref[pl.ds(row, BLK), :width] for row in picked], axis=0)
        values = jnp.concatenate([kv_ref[pl.ds(row, BLK), width:] for row in picked], axis=0)
        scores = lax.dot_general(
            both, keys, (((1,), (1,)), ((), ())), preferred_element_type=jnp.float32
        )
        slot_of = lax.broadcasted_iota(jnp.int32, (1, LMAX * BLK), 1) // BLK
        scores = scores + jnp.where(slot_of < counts_ref[block], 0.0, -jnp.inf)
        top = jnp.max(scores, axis=-1, keepdims=True)
        expo = jnp.exp(scores - top)
        total = jnp.sum(expo, axis=-1, keepdims=True)
        summed = jnp.dot(expo.astype(jnp.bfloat16), values, preferred_element_type=jnp.float32)
        summed = summed / total
        attended = jnp.where(first, summed[:BLK], summed[BLK:]).astype(jnp.bfloat16)
        stream = query + attended.astype(jnp.float32)
        out_ref[:, block] = stream.astype(jnp.bfloat16).reshape(parts, part_rows, width)


def attend_kernel(per, *refs):
    steps = refs[2].shape[0] // per
    lax.fori_loop(0, steps, lambda step, _: attend_step(step, per, *refs), None)


def attend(query, kv, cells, counts, parts, per):
    blocks, _, width = query.shape
    return pl.pallas_call(
        functools.partial(attend_kernel, per),
        out_shape=pltpu.VMEM((parts, blocks, BLK // parts, width), jnp.bfloat16),
        in_specs=[pl.BlockSpec(memory_space=pltpu.SMEM)] * 2
        + [pl.BlockSpec(memory_space=pltpu.VMEM)] * 2,
        name="attend",
    )(cells, counts, *on_chip(query, kv))


def flux_kernel(stream_ref, gain_ref, up_ref, flux_ref, out_ref):
    groups = stream_ref.shape[0]
    stream = jnp.concatenate(
        [stream_ref[h].astype(jnp.float32) for h in range(groups)], axis=1
    )
    scale = lax.rsqrt(jnp.mean(stream * stream, axis=-1, keepdims=True) + 1e-06)
    normed = (stream * scale * gain_ref[...]).astype(jnp.bfloat16)
    hidden = jax.nn.gelu(
        jnp.dot(normed, up_ref[...], preferred_element_type=jnp.float32)
    ).astype(jnp.bfloat16)
    flux = lax.dot_general(
        flux_ref[...], hidden, (((1,), (1,)), ((), ())), preferred_element_type=jnp.float32
    )
    blocks = out_ref.shape[0]
    few = flux.shape[1] // blocks
    for block in range(blocks):
        piece = flux[:, block * few : (block + 1) * few]
        out_ref[block] = jnp.concatenate([piece] * (LANES // few), axis=1)


def wall_flux(stream, norm_gain, up_weight, flux_weight, blocks):
    return pl.pallas_call(
        flux_kernel,
        out_shape=pltpu.VMEM((blocks, flux_weight.shape[0], LANES), jnp.float32),
        in_specs=[pl.BlockSpec(memory_space=pltpu.VMEM)] * 4,
        name="wall_flux",
    )(*on_chip(stream, norm_gain[None, :], up_weight, flux_weight))


def place_kernel(flux_ref, out_ref):
    _, halves, n_y, both, _ = flux_ref.shape
    comps, rows = out_ref.shape
    few = rows * comps // (halves * n_y * both)
    mine = flux_ref.at[lax.axis_index("y")]
    pieces = [
        mine[half, low, top * comps : (top + 1) * comps, :few]
        for top in range(both // comps)
        for low in range(n_y)
        for half in range(halves)
    ]
    out_ref[...] = jnp.concatenate(pieces, axis=1)


def place_flux(flux, comps, rows):
    return pl.pallas_call(
        place_kernel,
        out_shape=jax.ShapeDtypeStruct((comps, rows), jnp.float32),
        in_specs=[pl.BlockSpec(memory_space=pltpu.VMEM)],
        name="place_flux",
    )(*on_chip(flux))


def body(
    sizes,
    anchor_states,
    key_weight,
    value_weight,
    panel_query,
    cell_list,
    cell_count,
    norm_gain,
    up_weight,
    flux_weight,
):
    n_x, n_z, n_y = sizes
    grp = 2 * n_x
    width = key_weight.shape[1]
    hi = n_z // grp
    query = panel_query.reshape(hi, n_y, SLAB, grp, width).transpose(3, 1, 0, 2, 4)
    query = exchange(query.reshape(grp * n_y, hi * SLAB, width), PLANE)
    query = query.reshape(grp, n_y, hi, SLAB, width).transpose(0, 2, 1, 3, 4)
    query = query.reshape(n_z, n_y * SLAB, width)
    query = exchange(query, "z")
    up = [((i + 1) % n_x, i) for i in range(n_x)]
    down = [(i, (i + 1) % n_x) for i in range(n_x)]
    one_up = lax.ppermute(anchor_states, "x", up)
    one_down = lax.ppermute(anchor_states, "x", down)
    two_up = lax.ppermute(one_up, "x", up)
    along = jnp.concatenate([anchor_states, one_up, two_up, one_down], axis=0)
    across = lax.ppermute(along, "core", [(0, 1), (1, 0)])
    weights = jnp.concatenate([key_weight, value_weight], axis=1)
    kv = jnp.concatenate(
        [
            jnp.dot(part, weights, preferred_element_type=jnp.float32).astype(jnp.bfloat16)
            for part in (along, across)
        ],
        axis=0,
    )
    stream = attend(query, kv, cell_list.T, cell_count, grp, 16)
    stream = exchange(stream, GRP)
    flux = wall_flux(
        stream.reshape(grp, -1, width), norm_gain, up_weight, flux_weight, n_z
    )
    comps = flux_weight.shape[0]
    flux = exchange(flux, "z").reshape(grp, 1, hi * comps, LANES)
    flux = jnp.broadcast_to(flux, (grp, n_y, hi * comps, LANES))
    flux = exchange(flux.reshape(grp * n_y, hi * comps, LANES), PLANE)
    return place_flux(
        flux.reshape(n_x, 2, n_y, hi * comps, LANES), comps, panel_query.shape[0]
    )


def solution(mesh):
    grp, wide = mesh.devices.shape
    sizes = (grp // 2, 16, wide // 16)
    fine = Mesh(mesh.devices.reshape(grp // 2, 2, 16, wide // 16), ("x", "core", "z", "y"))
    rows = ("z", "y", "x", "core")
    in_specs = (
        P(rows, None),
        P(None, GRP),
        P(None, GRP),
        P(rows, None),
        P(("z", "y"), None),
        P(("z", "y")),
        P(),
        P(),
        P(),
    )
    return jax.shard_map(
        functools.partial(body, sizes),
        mesh=fine,
        in_specs=in_specs,
        out_specs=P(None, rows),
        check_vma=False,
    )
```

```python
import functools
import math

import jax
import jax.numpy as jnp
from jax import lax
from jax.experimental import pallas as pl
from jax.experimental.pallas import tpu as pltpu
from jax.sharding import Mesh
from jax.sharding import PartitionSpec as P

BLK = 128
LMAX = 4
HD = 64
SLAB = 32
LANES = 128
GRP = ("x", "core")
PLANE = ("x", "core", "y")


def exchange(array, axes):
    return lax.all_to_all(array, axes, split_axis=0, concat_axis=0, tiled=True)


def on_chip(*arrays):
    return [pltpu.with_memory_space_constraint(array, pltpu.VMEM) for array in arrays]


def attend_step(step, per, cells_ref, counts_ref, query_ref, kv_ref, out_ref):
    parts, _, part_rows, width = out_ref.shape
    cells = kv_ref.shape[0] // BLK
    x, core = lax.axis_index("x"), lax.axis_index("core")
    first = lax.broadcasted_iota(jnp.int32, (BLK, width), 1) < HD
    ones = jnp.ones((LMAX * BLK, width), jnp.bfloat16)
    for item in range(per):
        block = step * per + item
        query = query_ref[block].astype(jnp.float32)
        scaled = query * (1.0 / math.sqrt(HD))
        both = jnp.concatenate(
            [jnp.where(first, scaled, 0.0), jnp.where(first, 0.0, scaled)], axis=0
        ).astype(jnp.bfloat16)
        picked = []
        for slot in range(LMAX):
            cell = jnp.clip(cells_ref[slot, block], 0, cells - 1)
            far = (cell // 2 - x + cells) % (cells // 2)
            row = far + (cells // 2) * ((cell + core) % 2)
            picked.append(pl.multiple_of(row * BLK, BLK))
        keys = jnp.concatenate([kv_ref[pl.ds(row, BLK), :width] for row in picked], axis=0)
        values = jnp.concatenate([kv_ref[pl.ds(row, BLK), width:] for row in picked], axis=0)
        scores = lax.dot_general(
            both, keys, (((1,), (1,)), ((), ())), preferred_element_type=jnp.float32
        )
        slot_of = lax.broadcasted_iota(jnp.int32, (1, LMAX * BLK), 1) // BLK
        scores = scores + jnp.where(slot_of < counts_ref[block], 0.0, -jnp.inf)
        top = jnp.max(scores, axis=-1, keepdims=True)
        expo = jnp.exp(scores - top)
        summed = jnp.dot(
            expo.astype(jnp.bfloat16),
            jnp.concatenate([values, ones], axis=1),
            preferred_element_type=jnp.float32,
        )
        summed = summed[:, :width] / summed[:, width:]
        attended = jnp.where(first, summed[:BLK], summed[BLK:]).astype(jnp.bfloat16)
        stream = query + attended.astype(jnp.float32)
        out_ref[:, block] = stream.astype(jnp.bfloat16).reshape(parts, part_rows, width)


def attend_kernel(per, *refs):
    steps = refs[2].shape[0] // per
    lax.fori_loop(0, steps, lambda step, _: attend_step(step, per, *refs), None)


def attend(query, kv, cells, counts, parts, per):
    blocks, _, width = query.shape
    return pl.pallas_call(
        functools.partial(attend_kernel, per),
        out_shape=pltpu.VMEM((parts, blocks, BLK // parts, width), jnp.bfloat16),
        in_specs=[pl.BlockSpec(memory_space=pltpu.SMEM)] * 2
        + [pl.BlockSpec(memory_space=pltpu.VMEM)] * 2,
        name="attend",
    )(cells, counts, *on_chip(query, kv))


def flux_kernel(stream_ref, gain_ref, up_ref, flux_ref, out_ref):
    groups = stream_ref.shape[0]
    stream = jnp.concatenate(
        [stream_ref[h].astype(jnp.float32) for h in range(groups)], axis=1
    )
    scale = lax.rsqrt(jnp.mean(stream * stream, axis=-1, keepdims=True) + 1e-06)
    normed = (stream * scale * gain_ref[...]).astype(jnp.bfloat16)
    hidden = jax.nn.gelu(
        jnp.dot(normed, up_ref[...], preferred_element_type=jnp.float32)
    ).astype(jnp.bfloat16)
    flux = lax.dot_general(
        flux_ref[...], hidden, (((1,), (1,)), ((), ())), preferred_element_type=jnp.float32
    )
    blocks = out_ref.shape[0]
    few = flux.shape[1] // blocks
    for block in range(blocks):
        piece = flux[:, block * few : (block + 1) * few]
        out_ref[block] = jnp.concatenate([piece] * (LANES // few), axis=1)


def wall_flux(stream, norm_gain, up_weight, flux_weight, blocks):
    return pl.pallas_call(
        flux_kernel,
        out_shape=pltpu.VMEM((blocks, flux_weight.shape[0], LANES), jnp.float32),
        in_specs=[pl.BlockSpec(memory_space=pltpu.VMEM)] * 4,
        name="wall_flux",
    )(*on_chip(stream, norm_gain[None, :], up_weight, flux_weight))


def place_kernel(flux_ref, out_ref):
    _, halves, n_y, both, _ = flux_ref.shape
    comps, rows = out_ref.shape
    few = rows * comps // (halves * n_y * both)
    mine = flux_ref.at[lax.axis_index("y")]
    pieces = [
        mine[half, low, top * comps : (top + 1) * comps, :few]
        for top in range(both // comps)
        for low in range(n_y)
        for half in range(halves)
    ]
    out_ref[...] = jnp.concatenate(pieces, axis=1)


def place_flux(flux, comps, rows):
    return pl.pallas_call(
        place_kernel,
        out_shape=jax.ShapeDtypeStruct((comps, rows), jnp.float32),
        in_specs=[pl.BlockSpec(memory_space=pltpu.VMEM)],
        name="place_flux",
    )(*on_chip(flux))


def body(
    sizes,
    anchor_states,
    key_weight,
    value_weight,
    panel_query,
    cell_list,
    cell_count,
    norm_gain,
    up_weight,
    flux_weight,
):
    n_x, n_z, n_y = sizes
    grp = 2 * n_x
    width = key_weight.shape[1]
    hi = n_z // grp
    query = panel_query.reshape(hi, n_y, SLAB, grp, width).transpose(3, 1, 0, 2, 4)
    query = exchange(query.reshape(grp * n_y, hi * SLAB, width), PLANE)
    query = query.reshape(grp, n_y, hi, SLAB, width).transpose(0, 2, 1, 3, 4)
    query = query.reshape(n_z, n_y * SLAB, width)
    query = exchange(query, "z")
    up = [((i + 1) % n_x, i) for i in range(n_x)]
    down = [(i, (i + 1) % n_x) for i in range(n_x)]
    one_up = lax.ppermute(anchor_states, "x", up)
    one_down = lax.ppermute(anchor_states, "x", down)
    two_up = lax.ppermute(one_up, "x", up)
    along = jnp.concatenate([anchor_states, one_up, two_up, one_down], axis=0)
    across = lax.ppermute(along, "core", [(0, 1), (1, 0)])
    weights = jnp.concatenate([key_weight, value_weight], axis=1)
    kv = jnp.concatenate(
        [
            jnp.dot(part, weights, preferred_element_type=jnp.float32).astype(jnp.bfloat16)
            for part in (along, across)
        ],
        axis=0,
    )
    stream = attend(query, kv, cell_list.T, cell_count, grp, 16)
    stream = exchange(stream, GRP)
    flux = wall_flux(
        stream.reshape(grp, -1, width), norm_gain, up_weight, flux_weight, n_z
    )
    comps = flux_weight.shape[0]
    flux = exchange(flux, "z").reshape(grp, 1, hi * comps, LANES)
    flux = jnp.broadcast_to(flux, (grp, n_y, hi * comps, LANES))
    flux = exchange(flux.reshape(grp * n_y, hi * comps, LANES), PLANE)
    return place_flux(
        flux.reshape(n_x, 2, n_y, hi * comps, LANES), comps, panel_query.shape[0]
    )


def solution(mesh):
    grp, wide = mesh.devices.shape
    sizes = (grp // 2, 16, wide // 16)
    fine = Mesh(mesh.devices.reshape(grp // 2, 2, 16, wide // 16), ("x", "core", "z", "y"))
    rows = ("z", "y", "x", "core")
    in_specs = (
        P(rows, None),
        P(None, GRP),
        P(None, GRP),
        P(rows, None),
        P(("z", "y"), None),
        P(("z", "y")),
        P(),
        P(),
        P(),
    )
    return jax.shard_map(
        functools.partial(body, sizes),
        mesh=fine,
        in_specs=in_specs,
        out_specs=P(None, rows),
        check_vma=False,
    )
```

```python
import functools
import math

import jax
import jax.numpy as jnp
from jax import lax
from jax.experimental import pallas as pl
from jax.experimental.pallas import tpu as pltpu
from jax.sharding import Mesh
from jax.sharding import PartitionSpec as P

BLK = 128
LMAX = 4
HD = 64
SLAB = 32
LANES = 128
GRP = ("x", "core")
PLANE = ("x", "core", "y")


def exchange(array, axes):
    return lax.all_to_all(array, axes, split_axis=0, concat_axis=0, tiled=True)


def on_chip(*arrays):
    return [pltpu.with_memory_space_constraint(array, pltpu.VMEM) for array in arrays]


def project_kernel(along_ref, across_ref, keys_ref, values_ref, kv_ref):
    rows, width = along_ref.shape[0], keys_ref.shape[1]
    for start, ref in ((0, along_ref), (rows, across_ref)):
        for lane, weights_ref in ((0, keys_ref), (width, values_ref)):
            kv_ref[start : start + rows, lane : lane + width] = jnp.dot(
                ref[...], weights_ref[...], preferred_element_type=jnp.float32
            ).astype(jnp.bfloat16)


def project(along, across, keys, values):
    return pl.pallas_call(
        project_kernel,
        out_shape=pltpu.VMEM((2 * along.shape[0], 2 * keys.shape[1]), jnp.bfloat16),
        in_specs=[pl.BlockSpec(memory_space=pltpu.VMEM)] * 4,
        cost_estimate=pl.CostEstimate(flops=0, transcendentals=0, bytes_accessed=0),
        name="project",
    )(along, across, *on_chip(keys, values))


def attend_step(step, per, cells_ref, counts_ref, query_ref, kv_ref, out_ref):
    parts, _, part_rows, width = out_ref.shape
    cells = kv_ref.shape[0] // BLK
    x, core = lax.axis_index("x"), lax.axis_index("core")
    first = lax.broadcasted_iota(jnp.int32, (BLK, width), 1) < HD
    ones = jnp.ones((LMAX * BLK, width), jnp.bfloat16)
    for item in range(per):
        block = step * per + item
        query = query_ref[block].astype(jnp.float32)
        scaled = query * (1.0 / math.sqrt(HD))
        both = jnp.concatenate(
            [jnp.where(first, scaled, 0.0), jnp.where(first, 0.0, scaled)], axis=0
        ).astype(jnp.bfloat16)
        picked = []
        for slot in range(LMAX):
            cell = jnp.clip(cells_ref[slot, block], 0, cells - 1)
            far = (cell // 2 - x + cells) % (cells // 2)
            row = far + (cells // 2) * ((cell + core) % 2)
            picked.append(pl.multiple_of(row * BLK, BLK))
        keys = jnp.concatenate([kv_ref[pl.ds(row, BLK), :width] for row in picked], axis=0)
        values = jnp.concatenate([kv_ref[pl.ds(row, BLK), width:] for row in picked], axis=0)
        scores = lax.dot_general(
            both, keys, (((1,), (1,)), ((), ())), preferred_element_type=jnp.float32
        )
        slot_of = lax.broadcasted_iota(jnp.int32, (1, LMAX * BLK), 1) // BLK
        scores = scores + jnp.where(slot_of < counts_ref[block], 0.0, -jnp.inf)
        top = jnp.max(scores, axis=-1, keepdims=True)
        expo = jnp.exp(scores - top)
        summed = jnp.dot(
            expo.astype(jnp.bfloat16),
            jnp.concatenate([values, ones], axis=1),
            preferred_element_type=jnp.float32,
        )
        summed = summed[:, :width] / summed[:, width:]
        attended = jnp.where(first, summed[:BLK], summed[BLK:]).astype(jnp.bfloat16)
        stream = query + attended.astype(jnp.float32)
        out_ref[:, block] = stream.astype(jnp.bfloat16).reshape(parts, part_rows, width)


def attend_kernel(per, *refs):
    steps = refs[2].shape[0] // per
    lax.fori_loop(0, steps, lambda step, _: attend_step(step, per, *refs), None)


def attend(query, kv, cells, counts, parts, per):
    blocks, _, width = query.shape
    return pl.pallas_call(
        functools.partial(attend_kernel, per),
        out_shape=pltpu.VMEM((parts, blocks, BLK // parts, width), jnp.bfloat16),
        in_specs=[pl.BlockSpec(memory_space=pltpu.SMEM)] * 2
        + [pl.BlockSpec(memory_space=pltpu.VMEM)] * 2,
        name="attend",
    )(cells, counts, *on_chip(query, kv))


def flux_kernel(stream_ref, gain_ref, up_ref, flux_ref, out_ref):
    groups = stream_ref.shape[0]
    stream = jnp.concatenate(
        [stream_ref[h].astype(jnp.float32) for h in range(groups)], axis=1
    )
    scale = lax.rsqrt(jnp.mean(stream * stream, axis=-1, keepdims=True) + 1e-06)
    normed = (stream * scale * gain_ref[...]).astype(jnp.bfloat16)
    hidden = jax.nn.gelu(
        jnp.dot(normed, up_ref[...], preferred_element_type=jnp.float32)
    ).astype(jnp.bfloat16)
    flux = lax.dot_general(
        flux_ref[...], hidden, (((1,), (1,)), ((), ())), preferred_element_type=jnp.float32
    )
    blocks = out_ref.shape[0]
    few = flux.shape[1] // blocks
    for block in range(blocks):
        piece = flux[:, block * few : (block + 1) * few]
        out_ref[block] = jnp.concatenate([piece] * (LANES // few), axis=1)


def wall_flux(stream, norm_gain, up_weight, flux_weight, blocks):
    return pl.pallas_call(
        flux_kernel,
        out_shape=pltpu.VMEM((blocks, flux_weight.shape[0], LANES), jnp.float32),
        in_specs=[pl.BlockSpec(memory_space=pltpu.VMEM)] * 4,
        name="wall_flux",
    )(*on_chip(stream, norm_gain[None, :], up_weight, flux_weight))


def place_kernel(flux_ref, out_ref):
    _, halves, n_y, both, _ = flux_ref.shape
    comps, rows = out_ref.shape
    few = rows * comps // (halves * n_y * both)
    mine = flux_ref.at[lax.axis_index("y")]
    pieces = [
        mine[half, low, top * comps : (top + 1) * comps, :few]
        for top in range(both // comps)
        for low in range(n_y)
        for half in range(halves)
    ]
    out_ref[...] = jnp.concatenate(pieces, axis=1)


def place_flux(flux, comps, rows):
    return pl.pallas_call(
        place_kernel,
        out_shape=jax.ShapeDtypeStruct((comps, rows), jnp.float32),
        in_specs=[pl.BlockSpec(memory_space=pltpu.VMEM)],
        name="place_flux",
    )(*on_chip(flux))


def body(
    sizes,
    anchor_states,
    key_weight,
    value_weight,
    panel_query,
    cell_list,
    cell_count,
    norm_gain,
    up_weight,
    flux_weight,
):
    n_x, n_z, n_y = sizes
    grp = 2 * n_x
    width = key_weight.shape[1]
    hi = n_z // grp
    query = panel_query.reshape(hi, n_y, SLAB, grp, width).transpose(3, 1, 0, 2, 4)
    query = exchange(query.reshape(grp * n_y, hi * SLAB, width), PLANE)
    query = query.reshape(grp, n_y, hi, SLAB, width).transpose(0, 2, 1, 3, 4)
    query = query.reshape(n_z, n_y * SLAB, width)
    query, anchors = lax.optimization_barrier((query, anchor_states))
    query = exchange(query, "z")
    up = [((i + 1) % n_x, i) for i in range(n_x)]
    down = [(i, (i + 1) % n_x) for i in range(n_x)]
    one_up = lax.ppermute(anchors, "x", up)
    one_down = lax.ppermute(anchors, "x", down)
    one_up, one_down = lax.optimization_barrier((one_up, one_down))
    two_up = lax.ppermute(one_up, "x", up)
    along = jnp.concatenate([anchors, one_up, two_up, one_down], axis=0)
    across = lax.ppermute(along, "core", [(0, 1), (1, 0)])
    kv = project(along, across, key_weight, value_weight)
    stream = attend(query, kv, cell_list.T, cell_count, grp, 16)
    stream = exchange(stream, GRP)
    flux = wall_flux(
        stream.reshape(grp, -1, width), norm_gain, up_weight, flux_weight, n_z
    )
    comps = flux_weight.shape[0]
    flux = exchange(flux, "z").reshape(grp, 1, hi * comps, LANES)
    flux = jnp.broadcast_to(flux, (grp, n_y, hi * comps, LANES))
    flux = exchange(flux.reshape(grp * n_y, hi * comps, LANES), PLANE)
    return place_flux(
        flux.reshape(n_x, 2, n_y, hi * comps, LANES), comps, panel_query.shape[0]
    )


def solution(mesh):
    grp, wide = mesh.devices.shape
    sizes = (grp // 2, 16, wide // 16)
    fine = Mesh(mesh.devices.reshape(grp // 2, 2, 16, wide // 16), ("x", "core", "z", "y"))
    rows = ("z", "y", "x", "core")
    in_specs = (
        P(rows, None),
        P(None, GRP),
        P(None, GRP),
        P(rows, None),
        P(("z", "y"), None),
        P(("z", "y")),
        P(),
        P(),
        P(),
    )
    return jax.shard_map(
        functools.partial(body, sizes),
        mesh=fine,
        in_specs=in_specs,
        out_specs=P(None, rows),
        check_vma=False,
    )
```

```python
import functools
import math

import jax
import jax.numpy as jnp
from jax import lax
from jax.experimental import pallas as pl
from jax.experimental.pallas import tpu as pltpu
from jax.sharding import Mesh
from jax.sharding import PartitionSpec as P

BLK = 128
LMAX = 4
HD = 64
SLAB = 32
LANES = 128
GRP = ("x", "core")
PLANE = ("x", "core", "y")


def exchange(array, axes):
    return lax.all_to_all(array, axes, split_axis=0, concat_axis=0, tiled=True)


def on_chip(*arrays):
    return [pltpu.with_memory_space_constraint(array, pltpu.VMEM) for array in arrays]


def split_kernel(query_ref, out_ref):
    chunks, rows, width = out_ref.shape
    low = query_ref.shape[0] // rows
    for chunk in range(chunks):
        lane = chunk // low * width
        for top in range(rows // SLAB):
            row = (top * low + chunk % low) * SLAB
            out_ref[chunk, top * SLAB : (top + 1) * SLAB, :] = query_ref[
                row : row + SLAB, lane : lane + width
            ]


def split_query(query, groups, low):
    rows, width = query.shape
    steps = 2
    return pl.pallas_call(
        split_kernel,
        out_shape=jax.ShapeDtypeStruct((groups * low, rows // low, width // groups), query.dtype),
        grid=(steps,),
        in_specs=[pl.BlockSpec((rows, width // steps), lambda i: (0, i))],
        out_specs=pl.BlockSpec(
            (groups * low // steps, rows // low, width // groups), lambda i: (i, 0, 0)
        ),
        name="split_query",
    )(query)


def attend_step(step, per, cells_ref, counts_ref, query_ref, kv_ref, out_ref):
    parts, _, part_rows, width = out_ref.shape
    cells = kv_ref.shape[0] // BLK
    x, core = lax.axis_index("x"), lax.axis_index("core")
    first = lax.broadcasted_iota(jnp.int32, (BLK, width), 1) < HD
    ones = jnp.ones((LMAX * BLK, width), jnp.bfloat16)
    for item in range(per):
        block = step * per + item
        query = query_ref[block].astype(jnp.float32)
        scaled = query * (1.0 / math.sqrt(HD))
        both = jnp.concatenate(
            [jnp.where(first, scaled, 0.0), jnp.where(first, 0.0, scaled)], axis=0
        ).astype(jnp.bfloat16)
        picked = []
        for slot in range(LMAX):
            cell = jnp.clip(cells_ref[slot, block], 0, cells - 1)
            far = (cell // 2 - x + cells) % (cells // 2)
            row = far + (cells // 2) * ((cell + core) % 2)
            picked.append(pl.multiple_of(row * BLK, BLK))
        keys = jnp.concatenate([kv_ref[pl.ds(row, BLK), :width] for row in picked], axis=0)
        values = jnp.concatenate([kv_ref[pl.ds(row, BLK), width:] for row in picked], axis=0)
        scores = lax.dot_general(
            both, keys, (((1,), (1,)), ((), ())), preferred_element_type=jnp.float32
        )
        slot_of = lax.broadcasted_iota(jnp.int32, (1, LMAX * BLK), 1) // BLK
        scores = scores + jnp.where(slot_of < counts_ref[block], 0.0, -jnp.inf)
        top = jnp.max(scores, axis=-1, keepdims=True)
        expo = jnp.exp(scores - top)
        summed = jnp.dot(
            expo.astype(jnp.bfloat16),
            jnp.concatenate([values, ones], axis=1),
            preferred_element_type=jnp.float32,
        )
        summed = summed[:, :width] / summed[:, width:]
        attended = jnp.where(first, summed[:BLK], summed[BLK:]).astype(jnp.bfloat16)
        stream = query + attended.astype(jnp.float32)
        out_ref[:, block] = stream.astype(jnp.bfloat16).reshape(parts, part_rows, width)


def attend_kernel(per, *refs):
    steps = refs[2].shape[0] // per
    lax.fori_loop(0, steps, lambda step, _: attend_step(step, per, *refs), None)


def attend(query, kv, cells, counts, parts, per):
    blocks, _, width = query.shape
    return pl.pallas_call(
        functools.partial(attend_kernel, per),
        out_shape=pltpu.VMEM((parts, blocks, BLK // parts, width), jnp.bfloat16),
        in_specs=[pl.BlockSpec(memory_space=pltpu.SMEM)] * 2
        + [pl.BlockSpec(memory_space=pltpu.VMEM)] * 2,
        name="attend",
    )(cells, counts, *on_chip(query, kv))


def flux_kernel(stream_ref, gain_ref, up_ref, flux_ref, out_ref):
    groups = stream_ref.shape[0]
    stream = jnp.concatenate(
        [stream_ref[h].astype(jnp.float32) for h in range(groups)], axis=1
    )
    scale = lax.rsqrt(jnp.mean(stream * stream, axis=-1, keepdims=True) + 1e-06)
    normed = (stream * scale * gain_ref[...]).astype(jnp.bfloat16)
    hidden = jax.nn.gelu(
        jnp.dot(normed, up_ref[...], preferred_element_type=jnp.float32)
    ).astype(jnp.bfloat16)
    flux = lax.dot_general(
        flux_ref[...], hidden, (((1,), (1,)), ((), ())), preferred_element_type=jnp.float32
    )
    blocks = out_ref.shape[0]
    few = flux.shape[1] // blocks
    for block in range(blocks):
        piece = flux[:, block * few : (block + 1) * few]
        out_ref[block] = jnp.concatenate([piece] * (LANES // few), axis=1)


def wall_flux(stream, norm_gain, up_weight, flux_weight, blocks):
    return pl.pallas_call(
        flux_kernel,
        out_shape=pltpu.VMEM((blocks, flux_weight.shape[0], LANES), jnp.float32),
        in_specs=[pl.BlockSpec(memory_space=pltpu.VMEM)] * 4,
        name="wall_flux",
    )(*on_chip(stream, norm_gain[None, :], up_weight, flux_weight))


def place_kernel(flux_ref, out_ref):
    _, halves, n_y, both, _ = flux_ref.shape
    comps, rows = out_ref.shape
    few = rows * comps // (halves * n_y * both)
    mine = flux_ref.at[lax.axis_index("y")]
    pieces = [
        mine[half, low, top * comps : (top + 1) * comps, :few]
        for top in range(both // comps)
        for low in range(n_y)
        for half in range(halves)
    ]
    out_ref[...] = jnp.concatenate(pieces, axis=1)


def place_flux(flux, comps, rows):
    return pl.pallas_call(
        place_kernel,
        out_shape=jax.ShapeDtypeStruct((comps, rows), jnp.float32),
        in_specs=[pl.BlockSpec(memory_space=pltpu.VMEM)],
        name="place_flux",
    )(*on_chip(flux))


def body(
    sizes,
    anchor_states,
    key_weight,
    value_weight,
    panel_query,
    cell_list,
    cell_count,
    norm_gain,
    up_weight,
    flux_weight,
):
    n_x, n_z, n_y = sizes
    grp = 2 * n_x
    width = key_weight.shape[1]
    hi = n_z // grp
    query = exchange(split_query(panel_query, grp, n_y), PLANE)
    query = query.reshape(grp, n_y, hi, SLAB, width).transpose(0, 2, 1, 3, 4)
    query = query.reshape(n_z, n_y * SLAB, width)
    query = exchange(query, "z")
    up = [((i + 1) % n_x, i) for i in range(n_x)]
    down = [(i, (i + 1) % n_x) for i in range(n_x)]
    one_up = lax.ppermute(anchor_states, "x", up)
    one_down = lax.ppermute(anchor_states, "x", down)
    two_up = lax.ppermute(one_up, "x", up)
    along = jnp.concatenate([anchor_states, one_up, two_up, one_down], axis=0)
    across = lax.ppermute(along, "core", [(0, 1), (1, 0)])
    weights = jnp.concatenate([key_weight, value_weight], axis=1)
    kv = jnp.concatenate(
        [
            jnp.dot(part, weights, preferred_element_type=jnp.float32).astype(jnp.bfloat16)
            for part in (along, across)
        ],
        axis=0,
    )
    stream = attend(query, kv, cell_list.T, cell_count, grp, 16)
    stream = exchange(stream, GRP)
    flux = wall_flux(
        stream.reshape(grp, -1, width), norm_gain, up_weight, flux_weight, n_z
    )
    comps = flux_weight.shape[0]
    flux = exchange(flux, "z").reshape(grp, 1, hi * comps, LANES)
    flux = jnp.broadcast_to(flux, (grp, n_y, hi * comps, LANES))
    flux = exchange(flux.reshape(grp * n_y, hi * comps, LANES), PLANE)
    return place_flux(
        flux.reshape(n_x, 2, n_y, hi * comps, LANES), comps, panel_query.shape[0]
    )


def solution(mesh):
    grp, wide = mesh.devices.shape
    sizes = (grp // 2, 16, wide // 16)
    fine = Mesh(mesh.devices.reshape(grp // 2, 2, 16, wide // 16), ("x", "core", "z", "y"))
    rows = ("z", "y", "x", "core")
    in_specs = (
        P(rows, None),
        P(None, GRP),
        P(None, GRP),
        P(rows, None),
        P(("z", "y"), None),
        P(("z", "y")),
        P(),
        P(),
        P(),
    )
    return jax.shard_map(
        functools.partial(body, sizes),
        mesh=fine,
        in_specs=in_specs,
        out_specs=P(None, rows),
        check_vma=False,
    )
```

```python
import functools
import math

import jax
import jax.numpy as jnp
from jax import lax
from jax.experimental import pallas as pl
from jax.experimental.pallas import tpu as pltpu
from jax.sharding import Mesh
from jax.sharding import PartitionSpec as P

BLK = 128
LMAX = 4
HD = 64
SLAB = 32
LANES = 128
GRP = ("x", "core")
PLANE = ("x", "core", "y")


def exchange(array, axes):
    return lax.all_to_all(array, axes, split_axis=0, concat_axis=0, tiled=True)


def on_chip(*arrays):
    return [pltpu.with_memory_space_constraint(array, pltpu.VMEM) for array in arrays]


def split_kernel(query_ref, out_ref):
    chunks, rows, width = out_ref.shape
    low = query_ref.shape[0] // rows
    for chunk in range(chunks):
        lane = chunk // low * width
        for top in range(rows // SLAB):
            row = (top * low + chunk % low) * SLAB
            out_ref[chunk, top * SLAB : (top + 1) * SLAB, :] = query_ref[
                row : row + SLAB, lane : lane + width
            ]


def split_query(query, groups, low):
    rows, width = query.shape
    steps = 2
    return pl.pallas_call(
        split_kernel,
        out_shape=jax.ShapeDtypeStruct((groups * low, rows // low, width // groups), query.dtype),
        grid=(steps,),
        in_specs=[pl.BlockSpec((rows, width // steps), lambda i: (0, i))],
        out_specs=pl.BlockSpec(
            (groups * low // steps, rows // low, width // groups), lambda i: (i, 0, 0)
        ),
        name="split_query",
    )(query)


def attend_step(step, per, cells_ref, counts_ref, query_ref, kv_ref, out_ref):
    parts, _, part_rows, width = out_ref.shape
    cells = kv_ref.shape[0] // BLK
    x, core = lax.axis_index("x"), lax.axis_index("core")
    first = lax.broadcasted_iota(jnp.int32, (BLK, width), 1) < HD
    ones = jnp.ones((LMAX * BLK, width), jnp.bfloat16)
    for item in range(per):
        block = step * per + item
        query = query_ref[block].astype(jnp.float32)
        scaled = query * (1.0 / math.sqrt(HD))
        both = jnp.concatenate(
            [jnp.where(first, scaled, 0.0), jnp.where(first, 0.0, scaled)], axis=0
        ).astype(jnp.bfloat16)
        picked = []
        for slot in range(LMAX):
            cell = jnp.clip(cells_ref[slot, block], 0, cells - 1)
            far = (cell // 2 - x + cells) % (cells // 2)
            row = far + (cells // 2) * ((cell + core) % 2)
            picked.append(pl.multiple_of(row * BLK, BLK))
        keys = jnp.concatenate([kv_ref[pl.ds(row, BLK), :width] for row in picked], axis=0)
        values = jnp.concatenate([kv_ref[pl.ds(row, BLK), width:] for row in picked], axis=0)
        scores = lax.dot_general(
            both, keys, (((1,), (1,)), ((), ())), preferred_element_type=jnp.float32
        )
        slot_of = lax.broadcasted_iota(jnp.int32, (1, LMAX * BLK), 1) // BLK
        scores = scores + jnp.where(slot_of < counts_ref[block], 0.0, -jnp.inf)
        top = jnp.max(scores, axis=-1, keepdims=True)
        expo = jnp.exp(scores - top)
        summed = jnp.dot(
            expo.astype(jnp.bfloat16),
            jnp.concatenate([values, ones], axis=1),
            preferred_element_type=jnp.float32,
        )
        mine = jnp.where(first, summed[:BLK, :width], summed[BLK:, :width])
        total = jnp.where(first, summed[:BLK, width:], summed[BLK:, width:])
        attended = (mine / total).astype(jnp.bfloat16)
        stream = query + attended.astype(jnp.float32)
        out_ref[:, block] = stream.astype(jnp.bfloat16).reshape(parts, part_rows, width)


def attend_kernel(per, *refs):
    steps = refs[2].shape[0] // per
    lax.fori_loop(0, steps, lambda step, _: attend_step(step, per, *refs), None)


def attend(query, kv, cells, counts, parts, per):
    blocks, _, width = query.shape
    return pl.pallas_call(
        functools.partial(attend_kernel, per),
        out_shape=pltpu.VMEM((parts, blocks, BLK // parts, width), jnp.bfloat16),
        in_specs=[pl.BlockSpec(memory_space=pltpu.SMEM)] * 2
        + [pl.BlockSpec(memory_space=pltpu.VMEM)] * 2,
        name="attend",
    )(cells, counts, *on_chip(query, kv))


def flux_kernel(stream_ref, gain_ref, up_ref, flux_ref, out_ref):
    groups = stream_ref.shape[0]
    stream = jnp.concatenate(
        [stream_ref[h].astype(jnp.float32) for h in range(groups)], axis=1
    )
    scale = lax.rsqrt(jnp.mean(stream * stream, axis=-1, keepdims=True) + 1e-06)
    normed = (stream * scale * gain_ref[...]).astype(jnp.bfloat16)
    hidden = jax.nn.gelu(
        jnp.dot(normed, up_ref[...], preferred_element_type=jnp.float32)
    ).astype(jnp.bfloat16)
    flux = lax.dot_general(
        flux_ref[...], hidden, (((1,), (1,)), ((), ())), preferred_element_type=jnp.float32
    )
    blocks = out_ref.shape[0]
    few = flux.shape[1] // blocks
    for block in range(blocks):
        piece = flux[:, block * few : (block + 1) * few]
        out_ref[block] = jnp.concatenate([piece] * (LANES // few), axis=1)


def wall_flux(stream, norm_gain, up_weight, flux_weight, blocks):
    return pl.pallas_call(
        flux_kernel,
        out_shape=pltpu.VMEM((blocks, flux_weight.shape[0], LANES), jnp.float32),
        in_specs=[pl.BlockSpec(memory_space=pltpu.VMEM)] * 4,
        name="wall_flux",
    )(*on_chip(stream, norm_gain[None, :], up_weight, flux_weight))


def place_kernel(flux_ref, out_ref):
    _, halves, n_y, both, _ = flux_ref.shape
    comps, rows = out_ref.shape
    few = rows * comps // (halves * n_y * both)
    mine = flux_ref.at[lax.axis_index("y")]
    pieces = [
        mine[half, low, top * comps : (top + 1) * comps, :few]
        for top in range(both // comps)
        for low in range(n_y)
        for half in range(halves)
    ]
    out_ref[...] = jnp.concatenate(pieces, axis=1)


def place_flux(flux, comps, rows):
    return pl.pallas_call(
        place_kernel,
        out_shape=jax.ShapeDtypeStruct((comps, rows), jnp.float32),
        in_specs=[pl.BlockSpec(memory_space=pltpu.VMEM)],
        name="place_flux",
    )(*on_chip(flux))


def body(
    sizes,
    anchor_states,
    key_weight,
    value_weight,
    panel_query,
    cell_list,
    cell_count,
    norm_gain,
    up_weight,
    flux_weight,
):
    n_x, n_z, n_y = sizes
    grp = 2 * n_x
    width = key_weight.shape[1]
    hi = n_z // grp
    query = exchange(split_query(panel_query, grp, n_y), PLANE)
    query = query.reshape(grp, n_y, hi, SLAB, width).transpose(0, 2, 1, 3, 4)
    query = query.reshape(n_z, n_y * SLAB, width)
    query = exchange(query, "z")
    up = [((i + 1) % n_x, i) for i in range(n_x)]
    down = [(i, (i + 1) % n_x) for i in range(n_x)]
    one_up = lax.ppermute(anchor_states, "x", up)
    one_down = lax.ppermute(anchor_states, "x", down)
    two_up = lax.ppermute(one_up, "x", up)
    along = jnp.concatenate([anchor_states, one_up, two_up, one_down], axis=0)
    across = lax.ppermute(along, "core", [(0, 1), (1, 0)])
    weights = jnp.concatenate([key_weight, value_weight], axis=1)
    kv = jnp.concatenate(
        [
            jnp.dot(part, weights, preferred_element_type=jnp.float32).astype(jnp.bfloat16)
            for part in (along, across)
        ],
        axis=0,
    )
    stream = attend(query, kv, cell_list.T, cell_count, grp, 16)
    stream = exchange(stream, GRP)
    flux = wall_flux(
        stream.reshape(grp, -1, width), norm_gain, up_weight, flux_weight, n_z
    )
    comps = flux_weight.shape[0]
    flux = exchange(flux, "z").reshape(grp, 1, hi * comps, LANES)
    flux = jnp.broadcast_to(flux, (grp, n_y, hi * comps, LANES))
    flux = exchange(flux.reshape(grp * n_y, hi * comps, LANES), PLANE)
    return place_flux(
        flux.reshape(n_x, 2, n_y, hi * comps, LANES), comps, panel_query.shape[0]
    )


def solution(mesh):
    grp, wide = mesh.devices.shape
    sizes = (grp // 2, 16, wide // 16)
    fine = Mesh(mesh.devices.reshape(grp // 2, 2, 16, wide // 16), ("x", "core", "z", "y"))
    rows = ("z", "y", "x", "core")
    in_specs = (
        P(rows, None),
        P(None, GRP),
        P(None, GRP),
        P(rows, None),
        P(("z", "y"), None),
        P(("z", "y")),
        P(),
        P(),
        P(),
    )
    return jax.shard_map(
        functools.partial(body, sizes),
        mesh=fine,
        in_specs=in_specs,
        out_specs=P(None, rows),
        check_vma=False,
    )
```

```python
import functools
import math

import jax
import jax.numpy as jnp
from jax import lax
from jax.experimental import pallas as pl
from jax.experimental.pallas import tpu as pltpu
from jax.sharding import Mesh
from jax.sharding import PartitionSpec as P

BLK = 128
LMAX = 4
HD = 64
SLAB = 32
LANES = 128
GRP = ("x", "core")
PLANE = ("x", "core", "y")


def exchange(array, axes):
    return lax.all_to_all(array, axes, split_axis=0, concat_axis=0, tiled=True)


def on_chip(*arrays):
    return [pltpu.with_memory_space_constraint(array, pltpu.VMEM) for array in arrays]


def split_kernel(query_ref, out_ref):
    chunks, rows, width = out_ref.shape
    low = query_ref.shape[0] // rows
    for chunk in range(chunks):
        lane = chunk // low * width
        for top in range(rows // SLAB):
            row = (top * low + chunk % low) * SLAB
            out_ref[chunk, top * SLAB : (top + 1) * SLAB, :] = query_ref[
                row : row + SLAB, lane : lane + width
            ]


def split_query(query, groups, low):
    rows, width = query.shape
    steps = 2
    return pl.pallas_call(
        split_kernel,
        out_shape=jax.ShapeDtypeStruct((groups * low, rows // low, width // groups), query.dtype),
        grid=(steps,),
        in_specs=[pl.BlockSpec((rows, width // steps), lambda i: (0, i))],
        out_specs=pl.BlockSpec(
            (groups * low // steps, rows // low, width // groups), lambda i: (i, 0, 0)
        ),
        name="split_query",
    )(query)


def attend_step(step, per, cells_ref, counts_ref, query_ref, kv_ref, out_ref):
    parts, _, part_rows, width = out_ref.shape
    cells = kv_ref.shape[0] // BLK
    x, core = lax.axis_index("x"), lax.axis_index("core")
    first = lax.broadcasted_iota(jnp.int32, (BLK, width), 1) < HD
    ones = jnp.ones((LMAX * BLK, width), jnp.bfloat16)
    for item in range(per):
        block = step * per + item
        query = query_ref[block].astype(jnp.float32)
        scaled = query * (1.0 / math.sqrt(HD))
        both = jnp.concatenate(
            [jnp.where(first, scaled, 0.0), jnp.where(first, 0.0, scaled)], axis=0
        ).astype(jnp.bfloat16)
        picked = []
        for slot in range(LMAX):
            cell = jnp.clip(cells_ref[slot, block], 0, cells - 1)
            far = (cell // 2 - x + cells) % (cells // 2)
            row = far + (cells // 2) * ((cell + core) % 2)
            picked.append(pl.multiple_of(row * BLK, BLK))
        keys = jnp.concatenate([kv_ref[pl.ds(row, BLK), :width] for row in picked], axis=0)
        values = jnp.concatenate([kv_ref[pl.ds(row, BLK), width:] for row in picked], axis=0)
        scores = lax.dot_general(
            both, keys, (((1,), (1,)), ((), ())), preferred_element_type=jnp.float32
        )
        slot_of = lax.broadcasted_iota(jnp.int32, (1, LMAX * BLK), 1) // BLK
        scores = scores + jnp.where(slot_of < counts_ref[block], 0.0, -jnp.inf)
        top = jnp.max(scores, axis=-1, keepdims=True)
        expo = jnp.exp(scores - top)
        summed = jnp.dot(
            expo.astype(jnp.bfloat16),
            jnp.concatenate([values, ones], axis=1),
            preferred_element_type=jnp.float32,
        )
        mine = jnp.where(first, summed[:BLK, :width], summed[BLK:, :width])
        total = jnp.where(first, summed[:BLK, width:], summed[BLK:, width:])
        attended = (mine / total).astype(jnp.bfloat16)
        stream = query + attended.astype(jnp.float32)
        out_ref[:, block] = stream.astype(jnp.bfloat16).reshape(parts, part_rows, width)


def attend_kernel(per, *refs):
    steps = refs[2].shape[0] // per
    lax.fori_loop(0, steps, lambda step, _: attend_step(step, per, *refs), None)


def attend(query, kv, cells, counts, parts, per):
    blocks, _, width = query.shape
    return pl.pallas_call(
        functools.partial(attend_kernel, per),
        out_shape=pltpu.VMEM((parts, blocks, BLK // parts, width), jnp.bfloat16),
        in_specs=[pl.BlockSpec(memory_space=pltpu.SMEM)] * 2
        + [pl.BlockSpec(memory_space=pltpu.VMEM)] * 2,
        name="attend",
    )(cells, counts, *on_chip(query, kv))


def flux_kernel(stream_ref, gain_ref, up_ref, flux_ref, out_ref):
    groups, rows, _ = stream_ref.shape
    blocks = out_ref.shape[0]
    few = rows // blocks
    half = rows // 2
    for start in range(0, rows, half):
        stream = jnp.concatenate(
            [stream_ref[h, start : start + half].astype(jnp.float32) for h in range(groups)],
            axis=1,
        )
        scale = lax.rsqrt(jnp.mean(stream * stream, axis=-1, keepdims=True) + 1e-06)
        normed = (stream * scale * gain_ref[...]).astype(jnp.bfloat16)
        hidden = jax.nn.gelu(
            jnp.dot(normed, up_ref[...], preferred_element_type=jnp.float32)
        ).astype(jnp.bfloat16)
        flux = lax.dot_general(
            flux_ref[...], hidden, (((1,), (1,)), ((), ())), preferred_element_type=jnp.float32
        )
        for block in range(half // few):
            piece = flux[:, block * few : (block + 1) * few]
            out_ref[start // few + block] = jnp.concatenate([piece] * (LANES // few), axis=1)


def wall_flux(stream, norm_gain, up_weight, flux_weight, blocks):
    return pl.pallas_call(
        flux_kernel,
        out_shape=pltpu.VMEM((blocks, flux_weight.shape[0], LANES), jnp.float32),
        in_specs=[pl.BlockSpec(memory_space=pltpu.VMEM)] * 4,
        name="wall_flux",
    )(*on_chip(stream, norm_gain[None, :], up_weight, flux_weight))


def place_kernel(flux_ref, out_ref):
    _, halves, n_y, both, _ = flux_ref.shape
    comps, rows = out_ref.shape
    few = rows * comps // (halves * n_y * both)
    mine = flux_ref.at[lax.axis_index("y")]
    pieces = [
        mine[half, low, top * comps : (top + 1) * comps, :few]
        for top in range(both // comps)
        for low in range(n_y)
        for half in range(halves)
    ]
    out_ref[...] = jnp.concatenate(pieces, axis=1)


def place_flux(flux, comps, rows):
    return pl.pallas_call(
        place_kernel,
        out_shape=jax.ShapeDtypeStruct((comps, rows), jnp.float32),
        in_specs=[pl.BlockSpec(memory_space=pltpu.VMEM)],
        name="place_flux",
    )(*on_chip(flux))


def body(
    sizes,
    anchor_states,
    key_weight,
    value_weight,
    panel_query,
    cell_list,
    cell_count,
    norm_gain,
    up_weight,
    flux_weight,
):
    n_x, n_z, n_y = sizes
    grp = 2 * n_x
    width = key_weight.shape[1]
    hi = n_z // grp
    query = exchange(split_query(panel_query, grp, n_y), PLANE)
    query = query.reshape(grp, n_y, hi, SLAB, width).transpose(0, 2, 1, 3, 4)
    query = query.reshape(n_z, n_y * SLAB, width)
    query = exchange(query, "z")
    up = [((i + 1) % n_x, i) for i in range(n_x)]
    down = [(i, (i + 1) % n_x) for i in range(n_x)]
    one_up = lax.ppermute(anchor_states, "x", up)
    one_down = lax.ppermute(anchor_states, "x", down)
    two_up = lax.ppermute(one_up, "x", up)
    along = jnp.concatenate([anchor_states, one_up, two_up, one_down], axis=0)
    across = lax.ppermute(along, "core", [(0, 1), (1, 0)])
    weights = jnp.concatenate([key_weight, value_weight], axis=1)
    kv = jnp.concatenate(
        [
            jnp.dot(part, weights, preferred_element_type=jnp.float32).astype(jnp.bfloat16)
            for part in (along, across)
        ],
        axis=0,
    )
    stream = attend(query, kv, cell_list.T, cell_count, grp, 16)
    stream = exchange(stream, GRP)
    flux = wall_flux(
        stream.reshape(grp, -1, width), norm_gain, up_weight, flux_weight, n_z
    )
    comps = flux_weight.shape[0]
    flux = exchange(flux, "z").reshape(grp, 1, hi * comps, LANES)
    flux = jnp.broadcast_to(flux, (grp, n_y, hi * comps, LANES))
    flux = exchange(flux.reshape(grp * n_y, hi * comps, LANES), PLANE)
    return place_flux(
        flux.reshape(n_x, 2, n_y, hi * comps, LANES), comps, panel_query.shape[0]
    )


def solution(mesh):
    grp, wide = mesh.devices.shape
    sizes = (grp // 2, 16, wide // 16)
    fine = Mesh(mesh.devices.reshape(grp // 2, 2, 16, wide // 16), ("x", "core", "z", "y"))
    rows = ("z", "y", "x", "core")
    in_specs = (
        P(rows, None),
        P(None, GRP),
        P(None, GRP),
        P(rows, None),
        P(("z", "y"), None),
        P(("z", "y")),
        P(),
        P(),
        P(),
    )
    return jax.shard_map(
        functools.partial(body, sizes),
        mesh=fine,
        in_specs=in_specs,
        out_specs=P(None, rows),
        check_vma=False,
    )
```
